128 devices in a mesh: kv: 4 (over y), seq: 32 (over z, x, core).
Axes of the slice: x: 4, y: 4, z: 4, core: 2. Of those that a mesh axis runs over, the one named last changes fastest.
Arguments:
- queries: bfloat16 [32768, 4096], P('seq', 'kv'), may hold values from -40 to 40
- query_tangent: bfloat16 [32768, 4096], P('seq', 'kv'), may hold values from -6 to 6
- key_value: bfloat16 [32768, 2, 512], P('seq', None, 'kv'), may hold values from -40 to 40
- key_value_tangents: bfloat16 [32768, 2, 512], P('seq', None, 'kv'), may hold values from -6 to 6
- doc_lengths: int32 [256], replicated, may hold values from 1 to 1024, 32768 in all
- out_weight: bfloat16 [4096, 2048], P(('kv', 'seq')), may hold values from -1 to 1
- weight_tangent: bfloat16 [4096, 2048], P(('kv', 'seq')), may hold values from -0.25 to 0.25
Outputs:
- layer_out: bfloat16 [32768, 2048], P('seq', 'kv')
- out_tangent: bfloat16 [32768, 2048], P('seq', 'kv')
The draws below stay inside these ranges and needn't reach their ends.
Inputs may be any that keep to these rules, and one draw needn't show every extreme that they name: `doc_lengths`: the 256 lengths sum to 32768; the longest is exactly 1024.
All inputs are finite; a program needn't handle non-finite values.
Results may differ from the reference program's by a relative error of at most 0.0057.
Values may be sent and summed in bfloat16 or wider, within the bound.
A program may use at most 128 MiB of HBM per device.

```python
import math
import jax
import jax.numpy as jnp
import numpy as np
from jax import lax

D = 2048
QUERY_HEADS = 32
KEY_VALUE_HEADS = 4
HEAD_SIZE = 128
STRETCH = 32
WINDOW = 224
DOC_MOST = 1024
TOKEN_POSITIONS = 32768
NDOCS = 256


def shared_pair(key):
    base = jax.random.fold_in(key, 4711)
    query_random_key, key_value_pairs = jax.random.split(base, 2)
    heads_per_group = QUERY_HEADS // KEY_VALUE_HEADS
    query_sample = jax.random.normal(query_random_key, (TOKEN_POSITIONS, KEY_VALUE_HEADS, heads_per_group, HEAD_SIZE), jnp.float32)
    pair_sample = jax.random.normal(key_value_pairs, (TOKEN_POSITIONS, 2, KEY_VALUE_HEADS, HEAD_SIZE), jnp.float32)
    query_sample = jnp.clip(query_sample, -40.0, 40.0)
    pair_sample = jnp.clip(pair_sample, -40.0, 40.0)
    return (query_sample.reshape(TOKEN_POSITIONS, QUERY_HEADS * HEAD_SIZE), pair_sample.reshape(TOKEN_POSITIONS, 2, KEY_VALUE_HEADS * HEAD_SIZE))


def draw_queries(key, part):
    return shared_pair(key)[0].astype(jnp.bfloat16)


def draw_key_value(key, part):
    return shared_pair(key)[1].astype(jnp.bfloat16)


def with_spikes(values, rng, source, target, shards_of, factor):
    owner, partner = [(jnp.arange(values.shape[dim]) // (values.shape[dim] // shards_of)).reshape([-1 if axis == dim else 1 for axis in range(values.ndim)]) for dim in (source, target)]
    chosen = jax.random.permutation(rng, shards_of)[partner]
    strong = (owner == chosen) | (owner == (partner + shards_of // 2) % shards_of)
    return jnp.where(strong, factor * values, values)


def level_of(rng, extent, cuts, smallest, largest):
    factor_of = 1.0
    for dim, blocks in cuts:
        heights = jax.random.uniform(jax.random.fold_in(jax.random.fold_in(rng, 6), dim), (blocks,), jnp.float32, smallest / len(cuts), largest / len(cuts))
        factor_of = factor_of * jnp.repeat(jnp.exp(heights), extent[dim] // blocks).reshape((-1,) + (1,) * (len(extent) - 1 - dim))
    return factor_of


def profile(number_of, total, most, skew):
    loads = [(1 << 20) // math.isqrt(standing ** skew) + 1 for standing in range(2, number_of + 1)]
    spare, holding = total - most - (number_of - 1), [1] * (number_of - 1)
    while spare > 0:
        candidates = [i for i in range(number_of - 1) if holding[i] < most]
        mass, remaining = sum([loads[i] for i in candidates]), spare
        for i in candidates:
            more = min(most - holding[i], max(1, remaining * loads[i] // mass), spare)
            holding[i] = holding[i] + more
            spare = spare - more
    return np.array([most] + holding)


def uneven_parts(key, amount, total, bound, skew):
    if amount == 2:
        one = jax.random.randint(key, (), max(1, total - bound), min(bound, total - 1) + 1)
        return jnp.stack([one, total - one])
    tallies = jnp.asarray(profile(amount, total, bound, skew), jnp.int32)
    pairs = (amount - 1) // 2
    source_of, receiver = tallies[1:1 + 2 * pairs:2], tallies[2:2 + 2 * pairs:2]
    margin = jnp.minimum(source_of - 1, bound - receiver)
    shifted = jax.random.randint(jax.random.fold_in(key, 1), (pairs,), 0, 1 << 20) % (margin + 1)
    tallies = tallies.at[1:1 + 2 * pairs:2].set(source_of - shifted).at[2:2 + 2 * pairs:2].set(receiver + shifted)
    return tallies[jax.random.permutation(jax.random.fold_in(key, 2), amount)]


def normal_values(stream_key, extent, scale, most, cuts=(), held_as=jnp.bfloat16):
    array = scale * jax.random.normal(stream_key, extent, jnp.float32)
    if cuts:
        array = array * level_of(stream_key, extent, cuts, -0.22, 0.18)
    return jnp.clip(array, -most, most).astype(held_as)


def gaussian_with(rng, extent, deviation, reach, cuts, heavy, kind=jnp.bfloat16):
    values = deviation * jax.random.normal(rng, extent, jnp.float32)
    if cuts:
        values = values * level_of(rng, extent, cuts, -0.22, 0.18)
    return jnp.clip(with_spikes(values, jax.random.fold_in(rng, 3), *heavy), -reach, reach).astype(kind)


def setup_inputs(seed: int = 0) -> dict:
    streams_of = jax.random.split(jax.random.key(seed), 8)
    return {
        "queries": draw_queries(jax.random.fold_in(streams_of[7], 71), 0),
        "query_tangent": normal_values(streams_of[1], (TOKEN_POSITIONS, QUERY_HEADS * HEAD_SIZE), 1.0, 6.0, ((0, 32), (1, 4))),
        "key_value": draw_key_value(jax.random.fold_in(streams_of[7], 71), 0),
        "key_value_tangents": normal_values(streams_of[3], (TOKEN_POSITIONS, 2, KEY_VALUE_HEADS * HEAD_SIZE), 1.0, 6.0, ((0, 32), (2, 4))),
        "doc_lengths": uneven_parts(streams_of[4], NDOCS, TOKEN_POSITIONS, DOC_MOST, 2).astype(jnp.int32),
        "out_weight": gaussian_with(streams_of[5], (QUERY_HEADS * HEAD_SIZE, D), (QUERY_HEADS * HEAD_SIZE // 8) ** -0.5, 1.0, ((0, 128),), (0, 1, 128, 5.5)),
        "weight_tangent": normal_values(streams_of[6], (QUERY_HEADS * HEAD_SIZE, D), (QUERY_HEADS * HEAD_SIZE // 8) ** -0.5, 0.25, ((0, 128),)),
    }


masked_score = -1e+30

def attend(query_block, query_tan, key_rows, value_rows, key_tangent, value_tangent, lower_rel):
    head_dim = key_rows.shape[-1]
    score_scale = 1.0 / math.sqrt(head_dim)
    query_full = query_block.astype(jnp.float32)
    keys_full = key_rows.astype(jnp.float32)
    scores = jnp.einsum('bcgh,brh->bgcr', query_full, keys_full) * score_scale
    tangent = (jnp.einsum('bcgh,brh->bgcr', query_tan.astype(jnp.float32), keys_full) + jnp.einsum('bcgh,brh->bgcr', query_full, key_tangent.astype(jnp.float32))) * score_scale
    columns = jnp.arange(key_rows.shape[1]).astype(jnp.float32)[None, None, None, :]
    row_index = jnp.arange(query_block.shape[1]).astype(jnp.float32)[None, None, :, None]
    admitted = (columns >= lower_rel.astype(jnp.float32)[:, None, :, None]) & (columns <= row_index + WINDOW)
    scores = jnp.where(admitted, scores, masked_score)
    row_peak = lax.optimization_barrier(jnp.max(scores, axis=-1, keepdims=True))
    exponent = jnp.where(admitted, jnp.exp(scores - row_peak), 0.0)
    row_total = lax.optimization_barrier(jnp.sum(exponent, axis=-1, keepdims=True))
    probabilities = exponent / row_total
    tangent = jnp.where(admitted, tangent, 0.0)
    mean_tan = lax.optimization_barrier(jnp.sum(probabilities * tangent, axis=-1, keepdims=True))
    prob_tangent = probabilities * (tangent - mean_tan)
    prob_low = lax.optimization_barrier(probabilities.astype(jnp.bfloat16)).astype(jnp.float32)
    tangent_low = lax.optimization_barrier(prob_tangent.astype(jnp.bfloat16)).astype(jnp.float32)
    values_full = value_rows.astype(jnp.float32)
    outputs = jnp.einsum('bgcr,brh->bcgh', prob_low, values_full)
    out_tan = jnp.einsum('bgcr,brh->bcgh', tangent_low, values_full) + jnp.einsum('bgcr,brh->bcgh', prob_low, value_tangent.astype(jnp.float32))
    return (outputs.astype(jnp.bfloat16), out_tan.astype(jnp.bfloat16))

def reference(queries, query_tangent, key_value, key_value_tangents, doc_lengths, out_weight, weight_tangent):
    doc_ends = jnp.cumsum(doc_lengths).astype(jnp.int32)
    doc_starts = (doc_ends - doc_lengths).astype(jnp.int32)
    position = jnp.arange(TOKEN_POSITIONS, dtype=jnp.int32)
    inside = (doc_starts[None, :] <= position[:, None]) & (position[:, None] < doc_ends[None, :])
    doc_first = lax.optimization_barrier(jnp.sum(jnp.where(inside, doc_starts[None, :], 0), axis=1)).astype(jnp.int32)
    lower_bound = jnp.maximum(doc_first, position - WINDOW + 1).astype(jnp.int32)
    stretch_count = TOKEN_POSITIONS // STRETCH
    stretch_start = (jnp.arange(stretch_count, dtype=jnp.int32) * STRETCH)[:, None]
    lower_rel = (lower_bound.reshape(stretch_count, STRETCH) - (stretch_start - WINDOW)).astype(jnp.int32)
    heads_per_group = QUERY_HEADS // KEY_VALUE_HEADS
    span_count = (WINDOW + STRETCH) // STRETCH
    lead_blocks = WINDOW // STRETCH
    per_step = 32
    step_count = stretch_count // per_step
    attention_parts = []
    tangent_parts = []
    for group_number in range(KEY_VALUE_HEADS):
        low = group_number * HEAD_SIZE
        pair_rows = key_value[:, :, low:low + HEAD_SIZE]
        pair_tan = key_value_tangents[:, :, low:low + HEAD_SIZE]
        stacked = jnp.concatenate([pair_rows[:, 0], pair_rows[:, 1], pair_tan[:, 0], pair_tan[:, 1]], axis=1)
        padded = jnp.concatenate([jnp.zeros((WINDOW, 4 * HEAD_SIZE), jnp.bfloat16), stacked], axis=0)
        padded = padded.reshape(lead_blocks + stretch_count, STRETCH, 4 * HEAD_SIZE)
        windows = jnp.concatenate([padded[offset:offset + stretch_count] for offset in range(span_count)], axis=1)
        qlow = group_number * heads_per_group * HEAD_SIZE
        query_group = queries[:, qlow:qlow + heads_per_group * HEAD_SIZE].reshape(step_count, per_step, STRETCH, heads_per_group, HEAD_SIZE)
        tangent_group = query_tangent[:, qlow:qlow + heads_per_group * HEAD_SIZE].reshape(step_count, per_step, STRETCH, heads_per_group, HEAD_SIZE)
        window_group = windows.reshape(step_count, per_step, span_count * STRETCH, 4 * HEAD_SIZE)
        bound_group = lower_rel.reshape(step_count, per_step, STRETCH)

        def one_step(batch_items):
            query_batch, tangent_batch, window_batch, bound_batch = batch_items
            return attend(query_batch, tangent_batch, window_batch[..., :HEAD_SIZE], window_batch[..., HEAD_SIZE:2 * HEAD_SIZE], window_batch[..., 2 * HEAD_SIZE:3 * HEAD_SIZE], window_batch[..., 3 * HEAD_SIZE:], bound_batch)
        result = lax.map(one_step, (query_group, tangent_group, window_group, bound_group))
        attention_parts.append(result[0].reshape(TOKEN_POSITIONS, heads_per_group * HEAD_SIZE))
        tangent_parts.append(result[1].reshape(TOKEN_POSITIONS, heads_per_group * HEAD_SIZE))
    attention = jnp.concatenate(attention_parts, axis=1)
    attention_tan = jnp.concatenate(tangent_parts, axis=1)
    layer_out = jnp.dot(attention, out_weight, preferred_element_type=jnp.float32).astype(jnp.bfloat16)
    out_tangent = (jnp.dot(attention_tan, out_weight, preferred_element_type=jnp.float32) + jnp.dot(attention, weight_tangent, preferred_element_type=jnp.float32)).astype(jnp.bfloat16)
    return (layer_out, out_tangent)
```

```python
import math

import jax
import jax.numpy as jnp
from jax import lax
from jax.experimental import pallas as pl
from jax.experimental.pallas import tpu as pltpu
from jax.sharding import PartitionSpec as P

STRETCH = 32
WINDOW = 224
HEAD = 128
HEADS = 8
SPAN = WINDOW + STRETCH
MASKED = -1e30
SCALE = 1.0 / math.sqrt(HEAD)
EXP_SCALE = SCALE * math.log2(math.e)


def attend_block(q, qt, keys, values, lower_rel):
    rows = STRETCH * HEADS
    qs = jnp.concatenate([q[:, HEAD * h : HEAD * (h + 1)] for h in range(HEADS)], axis=0)
    qts = jnp.concatenate([qt[:, HEAD * h : HEAD * (h + 1)] for h in range(HEADS)], axis=0)
    dims = (((1,), (1,)), ((), ()))
    s = lax.dot_general(qs, keys[:, :HEAD], dims, preferred_element_type=jnp.float32)
    t = lax.dot_general(
        jnp.concatenate([qts, qs], axis=1), keys, dims, preferred_element_type=jnp.float32
    )
    column = lax.broadcasted_iota(jnp.int32, (STRETCH, SPAN), 1)
    row = lax.broadcasted_iota(jnp.int32, (STRETCH, SPAN), 0)
    admitted = (column >= lower_rel) & (column <= row + WINDOW)
    s = jnp.where(admitted[None], s.reshape(HEADS, STRETCH, SPAN), MASKED).reshape(rows, SPAN)
    peak = jnp.max(s, axis=-1, keepdims=True)
    e = jnp.exp2((s - peak) * EXP_SCALE)
    total = jnp.sum(e, axis=-1, keepdims=True)
    inverse = 1.0 / total
    mean = jnp.sum(e * t, axis=-1, keepdims=True) * inverse
    et = e * (t - mean)
    flat = (((1,), (0,)), ((), ()))
    ev = lax.dot_general(e.astype(jnp.bfloat16), values, flat, preferred_element_type=jnp.float32)
    etv = lax.dot_general(
        et.astype(jnp.bfloat16), values[:, :HEAD], flat, preferred_element_type=jnp.float32
    )
    out = (ev[:, :HEAD] * inverse).astype(jnp.bfloat16)
    tan = ((etv * SCALE + ev[:, HEAD:]) * inverse).astype(jnp.bfloat16)
    return out, tan


def attention_kernel(unroll, q_ref, qt_ref, keys_ref, values_ref, lower_ref, out_ref, tan_ref):
    blocks = q_ref.shape[0] // STRETCH

    def step(i, carry):
        at = pl.multiple_of(i * STRETCH, STRETCH)
        here = pl.ds(at, STRETCH)
        span = pl.ds(at, SPAN)
        out, tan = attend_block(
            q_ref[here, :], qt_ref[here, :], keys_ref[span, :], values_ref[span, :],
            lower_ref[here, :1],
        )
        for h in range(HEADS):
            out_ref[here, HEAD * h : HEAD * (h + 1)] = out[STRETCH * h : STRETCH * (h + 1)]
            tan_ref[here, HEAD * h : HEAD * (h + 1)] = tan[STRETCH * h : STRETCH * (h + 1)]
        return carry

    lax.fori_loop(0, blocks, step, 0, unroll=unroll)


def attention(q, qt, keys, values, lower_rel, unroll=2):
    import functools
    vmem = pl.BlockSpec(memory_space=pltpu.VMEM)
    shape = jax.ShapeDtypeStruct(q.shape, jnp.bfloat16)
    return pl.pallas_call(
        functools.partial(attention_kernel, unroll),
        out_shape=(shape, shape),
        in_specs=[vmem] * 5,
        out_specs=(vmem, vmem),
        compiler_params=pltpu.CompilerParams(vmem_limit_bytes=40 << 20),
        name="attention",
    )(q, qt, keys, values, lower_rel)


def passed_along(block, axis):
    n = lax.axis_size(axis)
    return lax.ppermute(block, axis, [(i, (i + 1) % n) for i in range(n)])


def body(
    queries, query_tangent, key_value, key_value_tangents, doc_lengths, out_weight, weight_tangent
):
    tokens = queries.shape[0]
    seq_index = lax.axis_index("seq")
    full_weight = lax.all_gather(out_weight, "seq", axis=0, tiled=True)
    full_tangent = lax.all_gather(weight_tangent, "seq", axis=0, tiled=True)
    stacked = jnp.concatenate(
        [key_value[:, 0], key_value_tangents[:, 0], key_value[:, 1], key_value_tangents[:, 1]],
        axis=1,
    )
    prior = passed_along(stacked[tokens - WINDOW :], "seq")
    context = jnp.concatenate([prior, stacked], axis=0)
    doc_ends = jnp.cumsum(doc_lengths)
    doc_starts = doc_ends - doc_lengths
    position = seq_index * tokens + jnp.arange(tokens, dtype=jnp.int32)
    doc_first = jnp.max(
        jnp.where(doc_starts[None, :] <= position[:, None], doc_starts[None, :], 0), axis=1
    )
    lower = jnp.maximum(doc_first, position - WINDOW + 1)
    lower_rel = lower - (position // STRETCH * STRETCH - WINDOW)
    lower_rel = jnp.broadcast_to(lower_rel[:, None], (tokens, 128))
    att, tan = attention(
        queries, query_tangent, context[:, : 2 * HEAD], context[:, 2 * HEAD :], lower_rel
    )
    part = jnp.dot(att, full_weight, preferred_element_type=jnp.float32).astype(jnp.bfloat16)
    part_tan = (
        jnp.dot(tan, full_weight, preferred_element_type=jnp.float32)
        + jnp.dot(att, full_tangent, preferred_element_type=jnp.float32)
    ).astype(jnp.bfloat16)
    return (
        lax.psum_scatter(part, "kv", scatter_dimension=1, tiled=True),
        lax.psum_scatter(part_tan, "kv", scatter_dimension=1, tiled=True),
    )


def solution(mesh):
    in_specs = (
        P("seq", "kv"),
        P("seq", "kv"),
        P("seq", None, "kv"),
        P("seq", None, "kv"),
        P(),
        P(("kv", "seq"), None),
        P(("kv", "seq"), None),
    )
    out_specs = (P("seq", "kv"), P("seq", "kv"))
    return jax.shard_map(body, mesh=mesh, in_specs=in_specs, out_specs=out_specs, check_vma=False)
```

```python
import math

import jax
import jax.numpy as jnp
from jax import lax
from jax.experimental import pallas as pl
from jax.experimental.pallas import tpu as pltpu
from jax.sharding import PartitionSpec as P

STRETCH = 32
WINDOW = 224
HEAD = 128
HEADS = 8
SPAN = WINDOW + STRETCH
MASKED = -1e30
SCALE = 1.0 / math.sqrt(HEAD)
EXP_SCALE = SCALE * math.log2(math.e)
MESH = pl.DeviceIdType.MESH

TOKENS = 1024
NDOCS = 256
GROUP = HEADS * HEAD
SHARE = 512
BLOCK = 256
BLOCKS = TOKENS // BLOCK
PAIR = 2 * STRETCH
STEPS = TOKENS // PAIR
RING = 4
ROWS = 32


def attend_block(q, qt, keys, values, starts, position):
    rows = STRETCH * HEADS
    qs = jnp.concatenate([q[:, HEAD * h : HEAD * (h + 1)] for h in range(HEADS)], axis=0)
    qts = jnp.concatenate([qt[:, HEAD * h : HEAD * (h + 1)] for h in range(HEADS)], axis=0)
    dims = (((1,), (1,)), ((), ()))
    s = lax.dot_general(qs, keys[:, :HEAD], dims, preferred_element_type=jnp.float32)
    t = lax.dot_general(
        jnp.concatenate([qts, qs], axis=1), keys, dims, preferred_element_type=jnp.float32
    )
    row = lax.broadcasted_iota(jnp.int32, (STRETCH, SPAN), 0)
    column = lax.broadcasted_iota(jnp.int32, (STRETCH, SPAN), 1)
    here = (position + row).astype(jnp.float32)
    first = jnp.max(jnp.where(starts <= here, starts, 0.0), axis=-1, keepdims=True)
    there = (position - WINDOW + column).astype(jnp.float32)
    admitted = (there >= first) & (there <= here) & (there > here - WINDOW)
    s = jnp.where(admitted[None], s.reshape(HEADS, STRETCH, SPAN), MASKED).reshape(rows, SPAN)
    peak = jnp.max(s, axis=-1, keepdims=True)
    e = jnp.exp2((s - peak) * EXP_SCALE)
    prob = e * (1.0 / jnp.sum(e, axis=-1, keepdims=True))
    t = t * SCALE
    mean = jnp.sum(prob * t, axis=-1, keepdims=True)
    prob_t = prob * (t - mean)
    flat = (((1,), (0,)), ((), ()))
    pv = lax.dot_general(prob.astype(jnp.bfloat16), values, flat, preferred_element_type=jnp.float32)
    tv = lax.dot_general(
        prob_t.astype(jnp.bfloat16), values[:, :HEAD], flat, preferred_element_type=jnp.float32
    )
    return pv[:, :HEAD].astype(jnp.bfloat16), (tv + pv[:, HEAD:]).astype(jnp.bfloat16)


def doc_starts(lengths):
    lane = lax.broadcasted_iota(jnp.int32, (8, NDOCS), 1)
    own = jnp.broadcast_to(lengths, (8, NDOCS))
    total = own
    shift = 1
    while shift < NDOCS:
        total = total + jnp.where(lane >= shift, pltpu.roll(total, shift, 1), 0)
        shift *= 2
    return (total - own).astype(jnp.float32)[:1]


def layer_kernel(
    lengths_ref, q_hbm, qt_hbm, kv_hbm, w_hbm, wt_hbm, out_hbm, tan_hbm,
    q_ref, qt_ref, ctx, w_ref, aa, d_out, d_in, m_out, m_in, own, final,
    load_sem, store_sem, halo_sem,
    one_send, one_recv, two_send, two_recv, three_send, three_recv, core_send, core_recv,
    d_send, d_recv, m_send, m_recv,
):
    y = lax.axis_index("kv")
    s = lax.axis_index("seq")
    z, x, c = s // 8, (s // 2) % RING, s % 2

    def seat(zz, xx, cc):
        return (y, lax.rem(zz, RING) * 8 + lax.rem(xx, RING) * 2 + cc)

    right, left = (lax.rem(y + 1, RING), s), (lax.rem(y + 3, RING), s)
    after, before = (y, lax.rem(s + 1, 32)), (y, lax.rem(s + 31, 32))
    partner = seat(z, x, 1 - c)

    def along(axis, distance):
        return seat(z, x + distance, c) if axis == 0 else seat(z + distance, x, c)

    loads = [
        pltpu.make_async_copy(kv_hbm, ctx.at[:, pl.ds(WINDOW, TOKENS)], load_sem.at[0]),
        pltpu.make_async_copy(q_hbm, q_ref, load_sem.at[1]),
        pltpu.make_async_copy(qt_hbm, qt_ref, load_sem.at[2]),
    ]
    for n in range(RING):
        share = lax.rem(y + (2, 1, 3, 0)[n], RING)
        columns = pl.ds(pl.multiple_of(share * SHARE, SHARE), SHARE)
        loads.append(
            pltpu.make_async_copy(w_hbm.at[:, columns], w_ref.at[n, 0, z, x, c], load_sem.at[3 + n])
        )
        loads.append(
            pltpu.make_async_copy(wt_hbm.at[:, columns], w_ref.at[n, 1, z, x, c], load_sem.at[7 + n])
        )
    for load in loads:
        load.start()

    barrier = pltpu.get_barrier_semaphore()
    greeted = [along(a, d) for a in (0, 1) for d in (1, 2, 3)]
    greeted += [partner, right, left, after, before]
    for device in greeted:
        pl.semaphore_signal(barrier, inc=1, device_id=device, device_id_type=MESH)
    pl.semaphore_wait(barrier, len(greeted))

    def remote(src, dst, send, recv, device):
        return pltpu.make_async_remote_copy(
            src_ref=src, dst_ref=dst, send_sem=send, recv_sem=recv,
            device_id=device, device_id_type=MESH,
        )

    def one(n, half):
        piece = w_ref.at[n, half, z, x, c]
        return [
            remote(piece, piece, one_send.at[n, half, d - 1], one_recv.at[n, half, d - 1],
                   along(half, d))
            for d in (1, 2, 3)
        ]

    def line(n, half, k, start=0, size=RING):
        part = pl.ds(start, size)
        return w_ref.at[n, 0, k, part, c] if half == 0 else w_ref.at[n, 1, part, k, c]

    def place(half):
        return z if half == 0 else x

    def two(n, half):
        mine = line(n, half, place(half))
        return [
            remote(mine, mine, two_send.at[n, half, j], two_recv.at[n, half, j],
                   along(1 - half, (1, 3)[j]))
            for j in (0, 1)
        ]

    def three(n, half):
        copies = []
        for j in (0, 1):
            k = lax.rem(place(half) + (3, 1)[j], RING)
            piece = line(n, half, k, 2 * j, 2)
            copies.append(
                remote(piece, piece, three_send.at[n, half, j], three_recv.at[n, half, j],
                       along(1 - half, (1, 3)[j]))
            )
        return copies

    def core(n, half, j):
        piece = line(n, half, lax.rem(place(half) + j, RING))
        return remote(piece, piece, core_send.at[n, half, j], core_recv.at[n, half, j], partner)

    halo = remote(
        kv_hbm.at[:, pl.ds(TOKENS - WINDOW, WINDOW)], ctx.at[:, pl.ds(0, WINDOW)],
        halo_sem.at[0], halo_sem.at[1], after,
    )

    def weights_one(n):
        for half in (0, 1):
            loads[3 + 2 * n + half].wait()
            for copy in one(n, half):
                copy.start()

    def weights_two(n):
        for half in (0, 1):
            for copy in one(n, half):
                copy.wait_recv()
            for copy in two(n, half):
                copy.start()
            core(n, half, 0).start()

    def weights_three(n):
        for half in (0, 1):
            for copy in two(n, half):
                copy.wait_recv()
            for copy in three(n, half):
                copy.start()
            core(n, half, 1).start()
            core(n, half, 3).start()

    def weights_four(n):
        for half in (0, 1):
            for copy in three(n, half):
                copy.wait_recv()
            core(n, half, 2).start()

    def weights_ready(n):
        for half in (0, 1):
            for j in range(RING):
                core(n, half, j).wait_recv()

    weights_one(0)
    halo.start()
    starts = doc_starts(lengths_ref[...])
    loads[0].wait()
    loads[1].wait()
    loads[2].wait()

    def order(b):
        return lax.rem(b + 1, BLOCKS)

    def attend_pair(i):
        for k in (0, 1):
            at = pl.multiple_of(lax.rem(i * PAIR + BLOCK, TOKENS) + k * STRETCH, STRETCH)
            here = pl.ds(at, STRETCH)
            span = pl.ds(at, SPAN)
            out, tan = attend_block(
                q_ref[here, :], qt_ref[here, :], ctx[0, span, :], ctx[1, span, :],
                starts, s * TOKENS + at,
            )
            for h in range(HEADS):
                rows = slice(STRETCH * h, STRETCH * (h + 1))
                aa[here, HEAD * h : HEAD * (h + 1)] = tan[rows]
                aa[here, GROUP + HEAD * h : GROUP + HEAD * (h + 1)] = out[rows]

    def project(b, n, put):
        here = pl.ds(pl.multiple_of(b * BLOCK, BLOCK), BLOCK)

        def tile(j, carry):
            columns = pl.ds(pl.multiple_of(j * 256, 256), 256)
            w = w_ref[n, 0, :, :, :, :, columns].reshape(GROUP, 256)
            wt = w_ref[n, 1, :, :, :, :, columns].reshape(GROUP, 256)
            att = aa[here, GROUP:]
            value = jnp.dot(att, w, preferred_element_type=jnp.float32)
            tan = jnp.dot(aa[here, :GROUP], w, preferred_element_type=jnp.float32)
            tan = tan + jnp.dot(att, wt, preferred_element_type=jnp.float32)
            put(columns, value, tan)
            return carry

        lax.fori_loop(0, SHARE // 256, tile, 0)

    def d_copy(b, j):
        return remote(d_out.at[b, j], d_in.at[b, j], d_send.at[b, j], d_recv.at[b, j],
                      (right, left)[j])

    def m_copy(b, j):
        return remote(m_out.at[b, j], m_in.at[b, j], m_send.at[b, j], m_recv.at[b, j],
                      (right, left)[j])

    def far(b):
        def put(columns, value, tan):
            d_out[b, 0, :, columns] = value.astype(jnp.bfloat16)
            d_out[b, 1, :, columns] = tan.astype(jnp.bfloat16)

        project(b, 0, put)
        d_copy(b, 0).start()
        d_copy(b, 1).start()

    def near(b, j):
        d_copy(b, j).wait_recv()

        def put(columns, value, tan):
            came = d_in[b, j, :, columns].astype(jnp.float32)
            if j == 0:
                value = value + came
            else:
                tan = tan + came
            m_out[b, j, 0, :, columns] = value.astype(jnp.bfloat16)
            m_out[b, j, 1, :, columns] = tan.astype(jnp.bfloat16)

        project(b, 1 + j, put)
        m_copy(b, j).start()

    def home(b):
        def put(columns, value, tan):
            own[b, 0, :, columns] = value
            own[b, 1, :, columns] = tan

        project(b, 3, put)

    def step(i, carry):
        @pl.when(i == 12)
        def _():
            halo.wait_recv()

        attend_pair(i)
        for n in range(RING):
            @pl.when(i == 3 * n + 1)
            def _():
                weights_two(n)
                if n + 1 < RING:
                    weights_one(n + 1)

            @pl.when(i == 3 * n + 4)
            def _():
                weights_three(n)

            @pl.when(i == min(3 * n + 6, STEPS - 1))
            def _():
                weights_four(n)

        return carry

    lax.fori_loop(0, STEPS, step, 0)
    weights_ready(0)

    def far_step(b, carry):
        far(order(b))
        return carry

    lax.fori_loop(0, BLOCKS, far_step, 0)
    weights_ready(1)
    weights_ready(2)

    def near_step(b, carry):
        near(order(b), 0)
        near(order(b), 1)
        return carry

    lax.fori_loop(0, BLOCKS, near_step, 0)
    weights_ready(3)

    def home_step(b, carry):
        home(order(b))
        return carry

    lax.fori_loop(0, BLOCKS, home_step, 0)

    def stores(b):
        here = pl.ds(pl.multiple_of(b * BLOCK, BLOCK), BLOCK)
        return [
            pltpu.make_async_copy(final.at[b, k], (out_hbm, tan_hbm)[k].at[here], store_sem.at[b, k])
            for k in (0, 1)
        ]

    def last_step(b, carry):
        b = order(b)
        m_copy(b, 0).wait_recv()
        m_copy(b, 1).wait_recv()
        for k in (0, 1):
            final[b, k] = (
                own[b, k]
                + m_in[b, 0, k].astype(jnp.float32)
                + m_in[b, 1, k].astype(jnp.float32)
            ).astype(jnp.bfloat16)
        for copy in stores(b):
            copy.start()
        return carry

    lax.fori_loop(0, BLOCKS, last_step, 0)

    def drain(b, carry):
        for j in (0, 1):
            d_copy(b, j).wait_send()
            m_copy(b, j).wait_send()
        for copy in stores(b):
            copy.wait()
        return carry

    lax.fori_loop(0, BLOCKS, drain, 0)
    halo.wait_send()
    for n in range(RING):
        for half in (0, 1):
            for copy in one(n, half) + two(n, half) + three(n, half):
                copy.wait_send()
            for j in range(RING):
                core(n, half, j).wait_send()


def layer(lengths, q, qt, kv, w, wt):
    anywhere = pl.BlockSpec(memory_space=pl.ANY)
    shape = jax.ShapeDtypeStruct((TOKENS, SHARE), jnp.bfloat16)
    bf16, f32 = jnp.bfloat16, jnp.float32
    dma = pltpu.SemaphoreType.DMA
    return pl.pallas_call(
        layer_kernel,
        out_shape=(shape, shape),
        in_specs=[pl.BlockSpec(memory_space=pltpu.VMEM)] + [anywhere] * 5,
        out_specs=(anywhere, anywhere),
        scratch_shapes=[
            pltpu.VMEM((TOKENS, GROUP), bf16),
            pltpu.VMEM((TOKENS, GROUP), bf16),
            pltpu.VMEM((2, WINDOW + TOKENS, 2 * HEAD), bf16),
            pltpu.VMEM((RING, 2, RING, RING, 2, ROWS, SHARE), bf16),
            pltpu.VMEM((TOKENS, 2 * GROUP), bf16),
            pltpu.VMEM((BLOCKS, 2, BLOCK, SHARE), bf16),
            pltpu.VMEM((BLOCKS, 2, BLOCK, SHARE), bf16),
            pltpu.VMEM((BLOCKS, 2, 2, BLOCK, SHARE), bf16),
            pltpu.VMEM((BLOCKS, 2, 2, BLOCK, SHARE), bf16),
            pltpu.VMEM((BLOCKS, 2, BLOCK, SHARE), f32),
            pltpu.VMEM((BLOCKS, 2, BLOCK, SHARE), bf16),
            dma((11,)),
            dma((BLOCKS, 2)),
            dma((2,)),
            dma((RING, 2, 3)),
            dma((RING, 2, 3)),
            dma((RING, 2, 2)),
            dma((RING, 2, 2)),
            dma((RING, 2, 2)),
            dma((RING, 2, 2)),
            dma((RING, 2, RING)),
            dma((RING, 2, RING)),
            dma((BLOCKS, 2)),
            dma((BLOCKS, 2)),
            dma((BLOCKS, 2)),
            dma((BLOCKS, 2)),
        ],
        compiler_params=pltpu.CompilerParams(
            collective_id=0, has_side_effects=True, vmem_limit_bytes=58 << 20
        ),
        name="layer",
    )(lengths, q, qt, kv, w, wt)


def body(
    queries, query_tangent, key_value, key_value_tangents, doc_lengths, out_weight, weight_tangent
):
    context = jnp.stack(
        [
            jnp.concatenate([key_value[:, k], key_value_tangents[:, k]], axis=1)
            for k in (0, 1)
        ]
    )
    return layer(
        doc_lengths[None, :], queries, query_tangent, context, out_weight, weight_tangent
    )


def solution(mesh):
    in_specs = (
        P("seq", "kv"),
        P("seq", "kv"),
        P("seq", None, "kv"),
        P("seq", None, "kv"),
        P(),
        P(("kv", "seq"), None),
        P(("kv", "seq"), None),
    )
    out_specs = (P("seq", "kv"), P("seq", "kv"))
    return jax.shard_map(body, mesh=mesh, in_specs=in_specs, out_specs=out_specs, check_vma=False)
```

```python
import functools
import math

import jax
import jax.numpy as jnp
from jax import lax
from jax.experimental import pallas as pl
from jax.experimental.pallas import tpu as pltpu
from jax.sharding import PartitionSpec as P

STRETCH = 32
WINDOW = 224
HEAD = 128
HEADS = 8
SPAN = WINDOW + STRETCH
MASKED = -1e30
SCALE = 1.0 / math.sqrt(HEAD)
EXP_SCALE = SCALE * math.log2(math.e)
MESH = pl.DeviceIdType.MESH

TOKENS = 1024
NDOCS = 256
GROUP = HEADS * HEAD
SHARE = 512
BLOCK = 256
BLOCKS = TOKENS // BLOCK
PAIR = 2 * STRETCH
STEPS = TOKENS // PAIR
RING = 4
ROWS = 32
PART = 256
PARTS = SHARE // PART
PIECES = RING * PARTS
VMEM_LIMIT = 44 << 20


def attend_block(q, qt, keys, values, starts, position):
    rows = STRETCH * HEADS
    qs = jnp.concatenate([q[:, HEAD * h : HEAD * (h + 1)] for h in range(HEADS)], axis=0)
    qts = jnp.concatenate([qt[:, HEAD * h : HEAD * (h + 1)] for h in range(HEADS)], axis=0)
    dims = (((1,), (1,)), ((), ()))
    s = lax.dot_general(qs, keys[:, :HEAD], dims, preferred_element_type=jnp.float32)
    t = lax.dot_general(
        jnp.concatenate([qts, qs], axis=1), keys, dims, preferred_element_type=jnp.float32
    )
    row = lax.broadcasted_iota(jnp.int32, (STRETCH, SPAN), 0)
    column = lax.broadcasted_iota(jnp.int32, (STRETCH, SPAN), 1)
    here = (position + row).astype(jnp.float32)
    first = jnp.max(jnp.where(starts <= here, starts, 0.0), axis=-1, keepdims=True)
    there = (position - WINDOW + column).astype(jnp.float32)
    admitted = (there >= first) & (there <= here) & (there > here - WINDOW)
    s = jnp.where(admitted[None], s.reshape(HEADS, STRETCH, SPAN), MASKED).reshape(rows, SPAN)
    peak = jnp.max(s, axis=-1, keepdims=True)
    e = jnp.exp2((s - peak) * EXP_SCALE)
    prob = e * (1.0 / jnp.sum(e, axis=-1, keepdims=True))
    t = t * SCALE
    mean = jnp.sum(prob * t, axis=-1, keepdims=True)
    prob_t = prob * (t - mean)
    flat = (((1,), (0,)), ((), ()))
    pv = lax.dot_general(prob.astype(jnp.bfloat16), values, flat, preferred_element_type=jnp.float32)
    tv = lax.dot_general(
        prob_t.astype(jnp.bfloat16), values[:, :HEAD], flat, preferred_element_type=jnp.float32
    )
    return pv[:, :HEAD].astype(jnp.bfloat16), (tv + pv[:, HEAD:]).astype(jnp.bfloat16)


def doc_starts(lengths):
    lane = lax.broadcasted_iota(jnp.int32, (8, NDOCS), 1)
    own = jnp.broadcast_to(lengths, (8, NDOCS))
    total = own
    shift = 1
    while shift < NDOCS:
        total = total + jnp.where(lane >= shift, pltpu.roll(total, shift, 1), 0)
        shift *= 2
    return (total - own).astype(jnp.float32)[:1]


def layer_kernel(
    lengths_ref, q_hbm, qt_hbm, kv_hbm, kvt_hbm, w_hbm, wt_hbm, out_ref, tan_ref,
    q_ref, qt_ref, raw, wide, ctx, w_ref, aa, d_out, d_in, m_out, m_in, own,
    load_sem, halo_sem, one_send, one_recv, two_send, two_recv, core_send, core_recv,
    d_send, d_recv, m_send, m_recv,
):
    y = lax.axis_index("kv")
    s = lax.axis_index("seq")
    z, x, c = s // 8, (s // 2) % RING, s % 2

    def seat(zz, xx, cc):
        return (y, lax.rem(zz, RING) * 8 + lax.rem(xx, RING) * 2 + cc)

    right, left = (lax.rem(y + 1, RING), s), (lax.rem(y + 3, RING), s)
    after, before = (y, lax.rem(s + 1, 32)), (y, lax.rem(s + 31, 32))
    partner = seat(z, x, 1 - c)

    def along(axis, distance):
        return seat(z, x + distance, c) if axis == 0 else seat(z + distance, x, c)

    def w_loads(n):
        share = lax.rem(y + (2, 1, 3, 0)[n // PARTS], RING)
        columns = pl.ds(pl.multiple_of(share * SHARE + n % PARTS * PART, PART), PART)
        return [
            pltpu.make_async_copy(w_hbm.at[:, columns], w_ref.at[n, 0, z, x, c], load_sem.at[4 + n]),
            pltpu.make_async_copy(
                wt_hbm.at[:, columns], w_ref.at[n, 1, z, x, c], load_sem.at[4 + PIECES + n]
            ),
        ]

    tail = pl.ds(2 * WINDOW, 2 * TOKENS)
    loads = [
        pltpu.make_async_copy(kv_hbm, raw.at[0, tail], load_sem.at[0]),
        pltpu.make_async_copy(kvt_hbm, raw.at[1, tail], load_sem.at[1]),
        pltpu.make_async_copy(q_hbm, q_ref, load_sem.at[2]),
        pltpu.make_async_copy(qt_hbm, qt_ref, load_sem.at[3]),
    ]
    for load in w_loads(0) + w_loads(1) + loads:
        load.start()
    for n in range(2, PIECES):
        for load in w_loads(n):
            load.start()

    barrier = pltpu.get_barrier_semaphore()
    greeted = [along(a, d) for a in (0, 1) for d in (1, 2, 3)]
    greeted += [partner, right, left, after, before]
    for device in greeted:
        pl.semaphore_signal(barrier, inc=1, device_id=device, device_id_type=MESH)
    pl.semaphore_wait(barrier, len(greeted))

    def remote(src, dst, send, recv, device):
        return pltpu.make_async_remote_copy(
            src_ref=src, dst_ref=dst, send_sem=send, recv_sem=recv,
            device_id=device, device_id_type=MESH,
        )

    def one(n, half):
        piece = w_ref.at[n, half, z, x, c]
        return [
            remote(piece, piece, one_send.at[n, half, d - 1], one_recv.at[n, half, d - 1],
                   along(half, d))
            for d in (1, 3, 2)
        ]

    def two(n, half):
        line = w_ref.at[n, 0, z, :, c] if half == 0 else w_ref.at[n, 1, :, x, c]
        return [
            remote(line, line, two_send.at[n, half, d - 1], two_recv.at[n, half, d - 1],
                   along(1 - half, d))
            for d in (1, 3, 2)
        ]

    def core(n):
        mine = w_ref.at[n, :, :, :, c]
        return remote(mine, mine, core_send.at[n], core_recv.at[n], partner)

    def weights_one(n):
        for load in w_loads(n):
            load.wait()
        for half in (0, 1):
            for copy in one(n, half):
                copy.start()

    def weights_two(n):
        for half in (0, 1):
            for copy in one(n, half):
                copy.wait_recv()
            for copy in two(n, half):
                copy.start()

    def weights_core(n):
        for half in (0, 1):
            for copy in two(n, half):
                copy.wait_recv()
        core(n).start()

    def weights_ready(n):
        core(n).wait_recv()

    def halo(k):
        return remote(
            (kv_hbm, kvt_hbm)[k].at[pl.ds(2 * (TOKENS - WINDOW), 2 * WINDOW)],
            raw.at[k, pl.ds(0, 2 * WINDOW)], halo_sem.at[k, 0], halo_sem.at[k, 1], after,
        )

    weights_one(0)
    weights_one(1)
    halo(0).start()
    halo(1).start()
    starts = doc_starts(lengths_ref[...])

    def unpack(at, rows):
        for k in (0, 1):
            wide[k, : 2 * rows] = raw[k, pl.ds(2 * at, 2 * rows)].astype(jnp.float32)
            for j in (0, 1):
                ctx[j, pl.ds(at, rows), HEAD * k : HEAD * (k + 1)] = wide[
                    k, pl.ds(j, rows, stride=2), :
                ].astype(jnp.bfloat16)

    loads[0].wait()
    loads[1].wait()

    def unpack_step(i, carry):
        unpack(pl.multiple_of(WINDOW + i * 128, 32), 128)
        return carry

    lax.fori_loop(0, TOKENS // 128, unpack_step, 0)
    loads[2].wait()
    loads[3].wait()

    def order(b):
        return lax.rem(b + 1, BLOCKS)

    def attend_pair(i):
        for k in (0, 1):
            at = pl.multiple_of(lax.rem(i * PAIR + BLOCK, TOKENS) + k * STRETCH, STRETCH)
            here = pl.ds(at, STRETCH)
            span = pl.ds(at, SPAN)
            out, tan = attend_block(
                q_ref[here, :], qt_ref[here, :], ctx[0, span, :], ctx[1, span, :],
                starts, s * TOKENS + at,
            )
            for h in range(HEADS):
                rows = slice(STRETCH * h, STRETCH * (h + 1))
                aa[here, HEAD * h : HEAD * (h + 1)] = tan[rows]
                aa[here, GROUP + HEAD * h : GROUP + HEAD * (h + 1)] = out[rows]

    def project(b, n):
        here = pl.ds(pl.multiple_of(b * BLOCK, BLOCK), BLOCK)
        w = w_ref[n, 0].reshape(GROUP, PART)
        wt = w_ref[n, 1].reshape(GROUP, PART)
        att = aa[here, GROUP:]
        value = jnp.dot(att, w, preferred_element_type=jnp.float32)
        tan = jnp.dot(aa[here, :GROUP], w, preferred_element_type=jnp.float32)
        tan = tan + jnp.dot(att, wt, preferred_element_type=jnp.float32)
        return value, tan

    def d_copy(b, p, j):
        return remote(d_out.at[b, p, j], d_in.at[b, p, j], d_send.at[b, p, j], d_recv.at[b, p, j],
                      (right, left)[j])

    def m_copy(b, p, j):
        return remote(m_out.at[b, p, j], m_in.at[b, p, j], m_send.at[b, p, j], m_recv.at[b, p, j],
                      (right, left)[j])

    def far(b, p):
        value, tan = project(b, p)
        d_out[b, p, 0] = value.astype(jnp.bfloat16)
        d_out[b, p, 1] = tan.astype(jnp.bfloat16)
        d_copy(b, p, 0).start()
        d_copy(b, p, 1).start()

    def near(b, p, j):
        value, tan = project(b, PARTS * (1 + j) + p)
        d_copy(b, p, j).wait_recv()
        came = d_in[b, p, j].astype(jnp.float32)
        if j == 0:
            value = value + came
        else:
            tan = tan + came
        m_out[b, p, j, 0] = value.astype(jnp.bfloat16)
        m_out[b, p, j, 1] = tan.astype(jnp.bfloat16)
        m_copy(b, p, j).start()

    def home(b, p):
        value, tan = project(b, PARTS * 3 + p)
        own[b, p, 0] = value
        own[b, p, 1] = tan

    plan = {i: [] for i in range(STEPS)}

    def at(i, action, *args):
        plan[i].append((action, args))

    at(0, weights_two, 0), at(0, weights_one, 2)
    at(2, weights_two, 1), at(2, weights_one, 3)
    at(5, weights_core, 0)
    at(5, weights_two, 2), at(5, weights_one, 4)
    at(6, weights_ready, 0), at(6, far, order(0), 0)
    at(7, far, order(1), 0)
    at(8, weights_core, 1)
    at(8, weights_two, 3), at(8, weights_one, 5)
    at(9, weights_ready, 1), at(9, far, order(0), 1)
    at(10, far, order(1), 1)
    at(11, far, order(2), 0)
    at(11, weights_core, 2)
    at(11, weights_two, 4), at(11, weights_one, 6)
    at(12, far, order(2), 1)
    at(13, weights_core, 3)
    at(13, weights_two, 5), at(13, weights_one, 7)

    fars = [(i, args) for i in plan for action, args in plan[i] if action is far]

    def step(i, carry):
        @pl.when(i == 12)
        def _():
            halo(0).wait_recv()
            halo(1).wait_recv()
            unpack(0, WINDOW)

        attend_pair(i)
        for k in range(STEPS):
            actions = [(f, a) for f, a in plan[k] if f is not far]
            if actions:
                @pl.when(i == k)
                def _():
                    for action, args in actions:
                        action(*args)

        hit = functools.reduce(jnp.logical_or, [i == k for k, _ in fars])

        @pl.when(hit)
        def _():
            b = sum(jnp.where(i == k, args[0], 0) for k, args in fars)
            p = sum(jnp.where(i == k, args[1], 0) for k, args in fars)
            far(b, p)

        return carry

    lax.fori_loop(0, STEPS, step, 0)
    weights_core(4)
    weights_two(6)
    weights_two(7)

    def last_far(p, carry):
        far(order(BLOCKS - 1), p)
        return carry

    lax.fori_loop(0, PARTS, last_far, 0)
    weights_ready(2)
    weights_ready(3)
    weights_core(5)
    weights_ready(4)
    weights_ready(5)

    def near_step(k, carry):
        near(order(k // PARTS), k % PARTS, 0)
        near(order(k // PARTS), k % PARTS, 1)
        return carry

    lax.fori_loop(0, BLOCKS * PARTS, near_step, 0)
    weights_core(6)
    weights_core(7)
    weights_ready(6)
    weights_ready(7)

    def home_step(k, carry):
        home(order(k // PARTS), k % PARTS)
        return carry

    lax.fori_loop(0, BLOCKS * PARTS, home_step, 0)

    def last_step(k, carry):
        b, p = order(k // PARTS), k % PARTS
        m_copy(b, p, 0).wait_recv()
        m_copy(b, p, 1).wait_recv()
        here = pl.ds(pl.multiple_of(b * BLOCK, BLOCK), BLOCK)
        columns = pl.ds(pl.multiple_of(p * PART, PART), PART)
        for j, ref in ((0, out_ref), (1, tan_ref)):
            ref[here, columns] = (
                own[b, p, j]
                + m_in[b, p, 0, j].astype(jnp.float32)
                + m_in[b, p, 1, j].astype(jnp.float32)
            ).astype(jnp.bfloat16)
        return carry

    lax.fori_loop(0, BLOCKS * PARTS, last_step, 0)

    def drain(k, carry):
        for j in (0, 1):
            d_copy(k // PARTS, k % PARTS, j).wait_send()
            m_copy(k // PARTS, k % PARTS, j).wait_send()
        return carry

    lax.fori_loop(0, BLOCKS * PARTS, drain, 0)
    halo(0).wait_send()
    halo(1).wait_send()
    for n in range(PIECES):
        for half in (0, 1):
            for copy in one(n, half) + two(n, half):
                copy.wait_send()
        core(n).wait_send()


def layer(lengths, q, qt, kv, kvt, w, wt):
    anywhere = pl.BlockSpec(memory_space=pltpu.HBM)
    vmem = pl.BlockSpec(memory_space=pltpu.VMEM)
    shape = jax.ShapeDtypeStruct((TOKENS, SHARE), jnp.bfloat16)
    bf16, f32 = jnp.bfloat16, jnp.float32
    dma = pltpu.SemaphoreType.DMA
    return pl.pallas_call(
        layer_kernel,
        out_shape=(shape, shape),
        in_specs=[vmem] + [anywhere] * 6,
        out_specs=(vmem, vmem),
        scratch_shapes=[
            pltpu.VMEM((TOKENS, GROUP), bf16),
            pltpu.VMEM((TOKENS, GROUP), bf16),
            pltpu.VMEM((2, 2 * (WINDOW + TOKENS), HEAD), bf16),
            pltpu.VMEM((2, 2 * WINDOW, HEAD), f32),
            pltpu.VMEM((2, WINDOW + TOKENS, 2 * HEAD), bf16),
            pltpu.VMEM((PIECES, 2, RING, RING, 2, ROWS, PART), bf16),
            pltpu.VMEM((TOKENS, 2 * GROUP), bf16),
            pltpu.VMEM((BLOCKS, PARTS, 2, BLOCK, PART), bf16),
            pltpu.VMEM((BLOCKS, PARTS, 2, BLOCK, PART), bf16),
            pltpu.VMEM((BLOCKS, PARTS, 2, 2, BLOCK, PART), bf16),
            pltpu.VMEM((BLOCKS, PARTS, 2, 2, BLOCK, PART), bf16),
            pltpu.VMEM((BLOCKS, PARTS, 2, BLOCK, PART), f32),
            dma((4 + 2 * PIECES,)),
            dma((2, 2)),
            dma((PIECES, 2, 3)),
            dma((PIECES, 2, 3)),
            dma((PIECES, 2, 3)),
            dma((PIECES, 2, 3)),
            dma((PIECES,)),
            dma((PIECES,)),
            dma((BLOCKS, PARTS, 2)),
            dma((BLOCKS, PARTS, 2)),
            dma((BLOCKS, PARTS, 2)),
            dma((BLOCKS, PARTS, 2)),
        ],
        compiler_params=pltpu.CompilerParams(
            collective_id=0, has_side_effects=True, vmem_limit_bytes=VMEM_LIMIT
        ),
        name="layer",
    )(lengths, q, qt, kv, kvt, w, wt)


def body(
    queries, query_tangent, key_value, key_value_tangents, doc_lengths, out_weight, weight_tangent
):
    hold = lambda v: pltpu.with_memory_space_constraint(v, pltpu.HBM)
    rows = 2 * TOKENS
    return layer(
        doc_lengths[None, :],
        hold(queries),
        hold(query_tangent),
        hold(key_value.reshape(rows, HEAD)),
        hold(key_value_tangents.reshape(rows, HEAD)),
        hold(out_weight),
        hold(weight_tangent),
    )


def solution(mesh):
    in_specs = (
        P("seq", "kv"),
        P("seq", "kv"),
        P("seq", None, "kv"),
        P("seq", None, "kv"),
        P(),
        P(("kv", "seq"), None),
        P(("kv", "seq"), None),
    )
    out_specs = (P("seq", "kv"), P("seq", "kv"))
    return jax.shard_map(body, mesh=mesh, in_specs=in_specs, out_specs=out_specs, check_vma=False)
```

```python
import functools
import math

import jax
import jax.numpy as jnp
from jax import lax
from jax.experimental import pallas as pl
from jax.experimental.pallas import tpu as pltpu
from jax.sharding import PartitionSpec as P

STRETCH = 32
WINDOW = 224
HEAD = 128
HEADS = 8
SPAN = WINDOW + STRETCH
MASKED = -1e30
SCALE = 1.0 / math.sqrt(HEAD)
EXP_SCALE = SCALE * math.log2(math.e)
MESH = pl.DeviceIdType.MESH

TOKENS = 1024
NDOCS = 256
GROUP = HEADS * HEAD
SHARE = 512
BLOCK = 256
BLOCKS = TOKENS // BLOCK
PAIR = 2 * STRETCH
STEPS = TOKENS // PAIR
RING = 4
ROWS = 32
PART = 256
PARTS = SHARE // PART
PIECES = RING * PARTS
VMEM_LIMIT = 44 << 20


def attend_block(q, qt, keys, values, starts, position):
    rows = STRETCH * HEADS
    qs = jnp.concatenate([q[:, HEAD * h : HEAD * (h + 1)] for h in range(HEADS)], axis=0)
    qts = jnp.concatenate([qt[:, HEAD * h : HEAD * (h + 1)] for h in range(HEADS)], axis=0)
    dims = (((1,), (1,)), ((), ()))
    s = lax.dot_general(qs, keys[:, :HEAD], dims, preferred_element_type=jnp.float32)
    t = lax.dot_general(
        jnp.concatenate([qts, qs], axis=1), keys, dims, preferred_element_type=jnp.float32
    )
    row = lax.broadcasted_iota(jnp.int32, (STRETCH, SPAN), 0)
    column = lax.broadcasted_iota(jnp.int32, (STRETCH, SPAN), 1)
    here = (position + row).astype(jnp.float32)
    first = jnp.max(jnp.where(starts <= here, starts, 0.0), axis=-1, keepdims=True)
    there = (position - WINDOW + column).astype(jnp.float32)
    admitted = (there >= first) & (there <= here) & (there > here - WINDOW)
    s = jnp.where(admitted[None], s.reshape(HEADS, STRETCH, SPAN), MASKED).reshape(rows, SPAN)
    peak = jnp.max(s, axis=-1, keepdims=True)
    e = jnp.exp2((s - peak) * EXP_SCALE)
    prob = e * (1.0 / jnp.sum(e, axis=-1, keepdims=True))
    t = t * SCALE
    mean = jnp.sum(prob * t, axis=-1, keepdims=True)
    prob_t = prob * (t - mean)
    flat = (((1,), (0,)), ((), ()))
    pv = lax.dot_general(prob.astype(jnp.bfloat16), values, flat, preferred_element_type=jnp.float32)
    tv = lax.dot_general(
        prob_t.astype(jnp.bfloat16), values[:, :HEAD], flat, preferred_element_type=jnp.float32
    )
    return pv[:, :HEAD].astype(jnp.bfloat16), (tv + pv[:, HEAD:]).astype(jnp.bfloat16)


def doc_starts(lengths):
    lane = lax.broadcasted_iota(jnp.int32, (8, NDOCS), 1)
    own = jnp.broadcast_to(lengths, (8, NDOCS))
    total = own
    shift = 1
    while shift < NDOCS:
        total = total + jnp.where(lane >= shift, pltpu.roll(total, shift, 1), 0)
        shift *= 2
    return (total - own).astype(jnp.float32)[:1]


def layer_kernel(
    lengths_hbm, q_hbm, qt_hbm, kv_hbm, kvt_hbm, w_hbm, wt_hbm, out_ref, tan_ref,
    lengths_ref, q_ref, qt_ref, raw, wide, ctx, w_ref, aa, d_out, d_in, m_out, m_in, own, final,
    kv_sem, q_sem, w_sem, halo_sem, first_send, first_recv, one_send, one_recv, two_send, two_recv, core_send, core_recv,
    d_send, d_recv, m_send, m_recv, out_sem,
):
    y = lax.axis_index("kv")
    s = lax.axis_index("seq")
    z, x, c = s // 8, (s // 2) % RING, s % 2

    def seat(zz, xx, cc):
        return (y, lax.rem(zz, RING) * 8 + lax.rem(xx, RING) * 2 + cc)

    right, left = (lax.rem(y + 1, RING), s), (lax.rem(y + 3, RING), s)
    after, before = (y, lax.rem(s + 1, 32)), (y, lax.rem(s + 31, 32))
    partner = seat(z, x, 1 - c)

    def along(axis, distance):
        return seat(z, x + distance, c) if axis == 0 else seat(z + distance, x, c)

    def w_loads(n):
        share = lax.rem(y + (2, 1, 3, 0)[n // PARTS], RING)
        columns = pl.ds(pl.multiple_of(share * SHARE + n % PARTS * PART, PART), PART)
        return [
            pltpu.make_async_copy(w_hbm.at[:, columns], w_ref.at[n, 0, z, x, c], w_sem.at[n]),
            pltpu.make_async_copy(wt_hbm.at[:, columns], w_ref.at[n, 1, z, x, c], w_sem.at[n]),
        ]

    barrier = pltpu.get_barrier_semaphore()
    steps = sorted(
        [(i, j) for i in range(RING) for j in range(RING) if i or j],
        key=lambda ij: -min(ij[0], RING - ij[0]) - min(ij[1], RING - ij[1]),
    )
    others = [seat(z + i, x + j, c) for i, j in steps]
    greeted = list(others)
    greeted += [right, left, after, before, partner]
    for device in greeted:
        pl.semaphore_signal(barrier, inc=1, device_id=device, device_id_type=MESH)

    def order(b):
        return lax.rem(b + 1, BLOCKS)

    tail = pl.ds(2 * WINDOW, 2 * TOKENS)
    kv_loads = [
        pltpu.make_async_copy(kv_hbm, raw.at[0, tail], kv_sem.at[0]),
        pltpu.make_async_copy(kvt_hbm, raw.at[1, tail], kv_sem.at[1]),
        pltpu.make_async_copy(lengths_hbm, lengths_ref, kv_sem.at[2]),
    ]

    def q_loads(k):
        here = pl.ds(pl.multiple_of(order(k) * BLOCK, BLOCK), BLOCK)
        return [
            pltpu.make_async_copy(q_hbm.at[here], q_ref.at[here], q_sem.at[k]),
            pltpu.make_async_copy(qt_hbm.at[here], qt_ref.at[here], q_sem.at[k]),
        ]

    for load in w_loads(0) + w_loads(1) + kv_loads + q_loads(0):
        load.start()
    for n in range(2, PIECES):
        for load in w_loads(n):
            load.start()
    for k in range(1, BLOCKS):
        for load in q_loads(k):
            load.start()
    def remote(src, dst, send, recv, device):
        return pltpu.make_async_remote_copy(
            src_ref=src, dst_ref=dst, send_sem=send, recv_sem=recv,
            device_id=device, device_id_type=MESH,
        )

    def one(n, half):
        piece = w_ref.at[n, half, z, x, c]
        return [
            remote(piece, piece, one_send.at[0], one_recv.at[n], along(half, d))
            for d in (2, 1, 3)
        ]

    def two(n, half):
        line = w_ref.at[n, 0, z, :, c] if half == 0 else w_ref.at[n, 1, :, x, c]
        return [
            remote(line, line, two_send.at[0], two_recv.at[n], along(1 - half, d))
            for d in (2, 1, 3)
        ]

    def core(n):
        mine = w_ref.at[n, :, :, :, c]
        return remote(mine, mine, core_send.at[0], core_recv.at[n], partner)

    def arrived(ref, sem):
        pltpu.make_async_copy(ref, ref, sem).wait()

    def weights_first():
        arrived(w_ref.at[0, :, 0, 0, 0], w_sem.at[0])
        mine = w_ref.at[0, :, z, x, c]
        for device in others:
            remote(mine, mine, first_send.at[0], first_recv.at[0], device).start()

    def core_first():
        arrived(w_ref.at[pl.ds(0, 5), 0, pl.ds(0, 3), 0], first_recv.at[0])
        core(0).start()

    def weights_one(n):
        arrived(w_ref.at[n, :, 0, 0, 0], w_sem.at[n])
        for half in (0, 1):
            for copy in one(n, half):
                copy.start()

    def weights_two(n):
        arrived(w_ref.at[n, 0, pl.ds(0, 3), 0], one_recv.at[n])
        for half in (0, 1):
            for copy in two(n, half):
                copy.start()

    def weights_core(n):
        arrived(w_ref.at[n, 0, pl.ds(0, 3)], two_recv.at[n])
        core(n).start()

    def weights_ready(n):
        core(n).wait_recv()

    def halo(k):
        return remote(
            (kv_hbm, kvt_hbm)[k].at[pl.ds(2 * (TOKENS - WINDOW), 2 * WINDOW)],
            raw.at[k, pl.ds(0, 2 * WINDOW)], halo_sem.at[0], halo_sem.at[1], after,
        )

    pl.semaphore_wait(barrier, len(greeted))
    weights_one(1)
    weights_first()
    weights_one(2)


    def unpack(at, rows):
        for k in (0, 1):
            wide[k, : 2 * rows] = raw[k, pl.ds(2 * at, 2 * rows)].astype(jnp.float32)
            for j in (0, 1):
                ctx[j, pl.ds(at, rows), HEAD * k : HEAD * (k + 1)] = wide[
                    k, pl.ds(j, rows, stride=2), :
                ].astype(jnp.bfloat16)

    for load in kv_loads:
        load.wait()
    starts = doc_starts(lengths_ref[...])

    def unpack_step(i, carry):
        unpack(pl.multiple_of(WINDOW + i * 128, 32), 128)
        return carry

    lax.fori_loop(0, TOKENS // 128, unpack_step, 0)
    def attend_pair(i):
        for k in (0, 1):
            at = pl.multiple_of(lax.rem(i * PAIR + BLOCK, TOKENS) + k * STRETCH, STRETCH)
            here = pl.ds(at, STRETCH)
            span = pl.ds(at, SPAN)
            out, tan = attend_block(
                q_ref[here, :], qt_ref[here, :], ctx[0, span, :], ctx[1, span, :],
                starts, s * TOKENS + at,
            )
            for h in range(HEADS):
                rows = slice(STRETCH * h, STRETCH * (h + 1))
                aa[here, HEAD * h : HEAD * (h + 1)] = tan[rows]
                aa[here, GROUP + HEAD * h : GROUP + HEAD * (h + 1)] = out[rows]

    def project(b, n):
        here = pl.ds(pl.multiple_of(b * BLOCK, BLOCK), BLOCK)
        w = w_ref[n, 0].reshape(GROUP, PART)
        wt = w_ref[n, 1].reshape(GROUP, PART)
        att = aa[here, GROUP:]
        value = jnp.dot(att, w, preferred_element_type=jnp.float32)
        tan = jnp.dot(aa[here, :GROUP], w, preferred_element_type=jnp.float32)
        tan = tan + jnp.dot(att, wt, preferred_element_type=jnp.float32)
        return value, tan

    def d_copy(b, p, j):
        return remote(d_out.at[b, p, j], d_in.at[b, p, j], d_send.at[0], d_recv.at[b, p, j],
                      (right, left)[j])

    def m_copy(b, p, j):
        return remote(m_out.at[b, p, j], m_in.at[b, p, j], m_send.at[0], m_recv.at[b, p, j],
                      (right, left)[j])

    def far(b, p):
        value, tan = project(b, p)
        d_out[b, p, 0] = value.astype(jnp.bfloat16)
        d_out[b, p, 1] = tan.astype(jnp.bfloat16)
        d_copy(b, p, 0).start()
        d_copy(b, p, 1).start()

    def near(b, p, j):
        value, tan = project(b, PARTS * (1 + j) + p)
        d_copy(b, p, j).wait_recv()
        came = d_in[b, p, j].astype(jnp.float32)
        if j == 0:
            value = value + came
        else:
            tan = tan + came
        m_out[b, p, j, 0] = value.astype(jnp.bfloat16)
        m_out[b, p, j, 1] = tan.astype(jnp.bfloat16)
        m_copy(b, p, j).start()

    def home(b, p):
        value, tan = project(b, PARTS * 3 + p)
        own[b, p, 0] = value
        own[b, p, 1] = tan

    plan = {i: [] for i in range(STEPS)}

    def at(i, action, *args):
        plan[i].append((action, args))

    def halo_start():
        halo(0).start()
        halo(1).start()

    at(1, halo_start)
    at(3, weights_one, 3), at(3, weights_two, 1)
    at(5, core_first), at(5, weights_ready, 0), at(5, far, order(0), 0)
    at(6, weights_one, 4), at(6, weights_two, 2)
    at(7, weights_core, 1), at(7, far, order(1), 0)
    at(8, weights_ready, 1), at(8, far, order(0), 1), at(8, weights_one, 5), at(8, weights_two, 3)
    at(9, far, order(1), 1)
    at(10, weights_one, 6), at(10, weights_two, 4), at(10, weights_core, 2)
    at(11, far, order(2), 0)
    at(12, far, order(2), 1), at(12, weights_one, 7), at(12, weights_two, 5)
    at(13, weights_core, 3)
    at(14, weights_two, 6)

    fars = [(i, args) for i in plan for action, args in plan[i] if action is far]

    def step(i, carry):
        @pl.when(i % 4 == 0)
        def _():
            arrived(aa.at[pl.ds(0, BLOCK)], q_sem.at[i // 4])

        @pl.when(i == 12)
        def _():
            arrived(raw.at[:, pl.ds(0, 2 * WINDOW)], halo_sem.at[1])
            unpack(0, WINDOW)

        attend_pair(i)

        def perform(wanted):
            for k in range(STEPS):
                actions = [(f, a) for f, a in plan[k] if f is not far and (f in (core_first, weights_ready)) == wanted]
                if actions:
                    @pl.when(i == k)
                    def _():
                        for action, args in actions:
                            action(*args)

        perform(True)

        hit = functools.reduce(jnp.logical_or, [i == k for k, _ in fars])

        @pl.when(hit)
        def _():
            b = sum(jnp.where(i == k, args[0], 0) for k, args in fars)
            p = sum(jnp.where(i == k, args[1], 0) for k, args in fars)
            far(b, p)

        perform(False)
        return carry

    lax.fori_loop(0, STEPS, step, 0)

    def last_far(p, carry):
        far(order(BLOCKS - 1), p)
        return carry

    lax.fori_loop(0, PARTS, last_far, 0)
    weights_two(7)
    weights_core(4)
    weights_ready(2)
    weights_ready(3)

    def near_step(k, carry):
        def right_step(p, carry):
            near(order(k), p, 0)
            return carry

        def left_step(p, carry):
            near(order(k), p, 1)
            return carry

        lax.fori_loop(0, PARTS, right_step, 0)

        @pl.when(k == 0)
        def _():
            weights_core(5)
            weights_ready(4)
            weights_ready(5)

        lax.fori_loop(0, PARTS, left_step, 0)

        @pl.when(k == 1)
        def _():
            weights_core(6)
            weights_core(7)

        return carry

    lax.fori_loop(0, BLOCKS, near_step, 0)
    weights_ready(6)
    weights_ready(7)

    def home_step(k, carry):
        home(order(k // PARTS), k % PARTS)
        return carry

    lax.fori_loop(0, BLOCKS * PARTS, home_step, 0)

    arrived(d_out, d_send.at[0])
    arrived(raw.at[:, pl.ds(0, 2 * WINDOW)], halo_sem.at[0])
    arrived(w_ref.at[pl.ds(0, 5), 0, pl.ds(0, 3), 0], first_send.at[0])
    arrived(w_ref.at[pl.ds(1, PIECES - 1), 0, pl.ds(0, 3), 0], one_send.at[0])
    arrived(w_ref.at[pl.ds(1, PIECES - 1), 0, pl.ds(0, 3)], two_send.at[0])
    arrived(w_ref.at[:, :, :, :, 0], core_send.at[0])

    def out_copy(b, p, j):
        here = pl.ds(pl.multiple_of(b * BLOCK, BLOCK), BLOCK)
        columns = pl.ds(pl.multiple_of(p * PART, PART), PART)
        return pltpu.make_async_copy(
            final.at[b, p, j], (out_ref, tan_ref)[j].at[here, columns], out_sem.at[0]
        )

    def last_step(k, carry):
        b, p = order(k // PARTS), k % PARTS
        m_copy(b, p, 0).wait_recv()
        m_copy(b, p, 1).wait_recv()
        for j in (0, 1):
            final[b, p, j] = (
                own[b, p, j]
                + m_in[b, p, 0, j].astype(jnp.float32)
                + m_in[b, p, 1, j].astype(jnp.float32)
            ).astype(jnp.bfloat16)
            out_copy(b, p, j).start()
        return carry

    lax.fori_loop(0, BLOCKS * PARTS, last_step, 0)

    arrived(m_out, m_send.at[0])
    arrived(final, out_sem.at[0])


def layer(lengths, q, qt, kv, kvt, w, wt):
    anywhere = pl.BlockSpec(memory_space=pltpu.HBM)
    shape = jax.ShapeDtypeStruct((TOKENS, SHARE), jnp.bfloat16)
    bf16, f32 = jnp.bfloat16, jnp.float32
    dma = pltpu.SemaphoreType.DMA
    return pl.pallas_call(
        layer_kernel,
        out_shape=(shape, shape),
        in_specs=[anywhere] * 7,
        out_specs=(pl.BlockSpec(memory_space=pl.ANY),) * 2,
        scratch_shapes=[
            pltpu.VMEM((1, NDOCS), jnp.int32),
            pltpu.VMEM((TOKENS, GROUP), bf16),
            pltpu.VMEM((TOKENS, GROUP), bf16),
            pltpu.VMEM((2, 2 * (WINDOW + TOKENS), HEAD), bf16),
            pltpu.VMEM((2, 2 * WINDOW, HEAD), f32),
            pltpu.VMEM((2, WINDOW + TOKENS, 2 * HEAD), bf16),
            pltpu.VMEM((PIECES, 2, RING, RING, 2, ROWS, PART), bf16),
            pltpu.VMEM((TOKENS, 2 * GROUP), bf16),
            pltpu.VMEM((BLOCKS, PARTS, 2, BLOCK, PART), bf16),
            pltpu.VMEM((BLOCKS, PARTS, 2, BLOCK, PART), bf16),
            pltpu.VMEM((BLOCKS, PARTS, 2, 2, BLOCK, PART), bf16),
            pltpu.VMEM((BLOCKS, PARTS, 2, 2, BLOCK, PART), bf16),
            pltpu.VMEM((BLOCKS, PARTS, 2, BLOCK, PART), f32),
            pltpu.VMEM((BLOCKS, PARTS, 2, BLOCK, PART), bf16),
            dma((3,)),
            dma((BLOCKS,)),
            dma((PIECES,)),
            dma((2,)),
            dma((1,)),
            dma((1,)),
            dma((1,)),
            dma((PIECES,)),
            dma((1,)),
            dma((PIECES,)),
            dma((1,)),
            dma((PIECES,)),
            dma((1,)),
            dma((BLOCKS, PARTS, 2)),
            dma((1,)),
            dma((BLOCKS, PARTS, 2)),
            dma((1,)),
        ],
        compiler_params=pltpu.CompilerParams(
            collective_id=0, has_side_effects=True, vmem_limit_bytes=VMEM_LIMIT
        ),
        name="layer",
    )(lengths, q, qt, kv, kvt, w, wt)


def flush_kernel(a_ref, b_ref, a_hbm, b_hbm, sem):
    copies = [
        pltpu.make_async_copy(a_ref, a_hbm, sem.at[0]),
        pltpu.make_async_copy(b_ref, b_hbm, sem.at[1]),
    ]
    for copy in copies:
        copy.start()
    for copy in copies:
        copy.wait()


def flush(a, b):
    anywhere, hbm = pl.BlockSpec(memory_space=pl.ANY), pl.BlockSpec(memory_space=pltpu.HBM)
    shape = jax.ShapeDtypeStruct(a.shape, a.dtype)
    return pl.pallas_call(
        flush_kernel,
        out_shape=(shape, shape),
        in_specs=[anywhere, anywhere],
        out_specs=(hbm, hbm),
        scratch_shapes=[pltpu.SemaphoreType.DMA((2,))],
        compiler_params=pltpu.CompilerParams(vmem_limit_bytes=4 << 20),
        name="flush",
    )(a, b)


def body(
    queries, query_tangent, key_value, key_value_tangents, doc_lengths, out_weight, weight_tangent
):
    hold = lambda v: pltpu.with_memory_space_constraint(v, pltpu.HBM)
    rows = 2 * TOKENS
    out, tan = layer(
        hold(doc_lengths[None, :]),
        hold(queries),
        hold(query_tangent),
        hold(key_value.reshape(rows, HEAD)),
        hold(key_value_tangents.reshape(rows, HEAD)),
        hold(out_weight),
        hold(weight_tangent),
    )
    return flush(out, tan)


def solution(mesh):
    in_specs = (
        P("seq", "kv"),
        P("seq", "kv"),
        P("seq", None, "kv"),
        P("seq", None, "kv"),
        P(),
        P(("kv", "seq"), None),
        P(("kv", "seq"), None),
    )
    out_specs = (P("seq", "kv"), P("seq", "kv"))
    return jax.shard_map(body, mesh=mesh, in_specs=in_specs, out_specs=out_specs, check_vma=False)
```

```python
import functools
import math

import jax
import jax.numpy as jnp
from jax import lax
from jax.experimental import pallas as pl
from jax.experimental.pallas import tpu as pltpu
from jax.sharding import PartitionSpec as P

STRETCH = 32
WINDOW = 224
HEAD = 128
HEADS = 8
SPAN = WINDOW + STRETCH
MASKED = -1e30
SCALE = 1.0 / math.sqrt(HEAD)
EXP_SCALE = SCALE * math.log2(math.e)
MESH = pl.DeviceIdType.MESH

TOKENS = 1024
NDOCS = 256
GROUP = HEADS * HEAD
SHARE = 512
BLOCK = 256
BLOCKS = TOKENS // BLOCK
TOGETHER = 4
STEP_ROWS = TOGETHER * STRETCH
STEPS = TOKENS // STEP_ROWS
RING = 4
ROWS = 32
PART = 256
PARTS = SHARE // PART
PIECES = RING * PARTS
VMEM_LIMIT = 44 << 20


def attend_block(q, qt, keys, values, starts, position):
    rows = STRETCH * HEADS
    qs = jnp.concatenate([q[:, HEAD * h : HEAD * (h + 1)] for h in range(HEADS)], axis=0)
    qts = jnp.concatenate([qt[:, HEAD * h : HEAD * (h + 1)] for h in range(HEADS)], axis=0)
    dims = (((1,), (1,)), ((), ()))
    s = lax.dot_general(qs, keys[:, :HEAD], dims, preferred_element_type=jnp.float32)
    t = lax.dot_general(
        jnp.concatenate([qts, qs], axis=1), keys, dims, preferred_element_type=jnp.float32
    )
    row = lax.broadcasted_iota(jnp.int32, (STRETCH, SPAN), 0)
    column = lax.broadcasted_iota(jnp.int32, (STRETCH, SPAN), 1)
    here = (position + row).astype(jnp.float32)
    first = jnp.max(jnp.where(starts <= here, starts, 0.0), axis=-1, keepdims=True)
    there = (position - WINDOW + column).astype(jnp.float32)
    admitted = (there >= first) & (there <= here) & (there > here - WINDOW)
    s = jnp.where(admitted[None], s.reshape(HEADS, STRETCH, SPAN), MASKED).reshape(rows, SPAN)
    peak = jnp.max(s, axis=-1, keepdims=True)
    e = jnp.exp2((s - peak) * EXP_SCALE)
    prob = e * (1.0 / jnp.sum(e, axis=-1, keepdims=True))
    t = t * SCALE
    mean = jnp.sum(prob * t, axis=-1, keepdims=True)
    prob_t = prob * (t - mean)
    flat = (((1,), (0,)), ((), ()))
    pv = lax.dot_general(prob.astype(jnp.bfloat16), values, flat, preferred_element_type=jnp.float32)
    tv = lax.dot_general(
        prob_t.astype(jnp.bfloat16), values[:, :HEAD], flat, preferred_element_type=jnp.float32
    )
    return pv[:, :HEAD].astype(jnp.bfloat16), (tv + pv[:, HEAD:]).astype(jnp.bfloat16)


def doc_starts(lengths):
    lane = lax.broadcasted_iota(jnp.int32, (8, NDOCS), 1)
    own = jnp.broadcast_to(lengths, (8, NDOCS))
    total = own
    shift = 1
    while shift < NDOCS:
        total = total + jnp.where(lane >= shift, pltpu.roll(total, shift, 1), 0)
        shift *= 2
    return (total - own).astype(jnp.float32)[:1]


def layer_kernel(
    lengths_hbm, q_hbm, qt_hbm, kv_hbm, kvt_hbm, w_hbm, wt_hbm, out_ref, tan_ref,
    lengths_ref, q_ref, qt_ref, raw, wide, ctx, w_ref, aa, d_out, d_in, m_out, m_in, own, final,
    kv_sem, q_sem, w_sem, halo_sem, first_send, first_recv, one_send, one_recv, two_send, two_recv, core_send, core_recv,
    d_send, d_recv, m_send, m_recv, out_sem,
):
    y = lax.axis_index("kv")
    s = lax.axis_index("seq")
    z, x, c = s // 8, (s // 2) % RING, s % 2

    def seat(zz, xx, cc):
        return (y, lax.rem(zz, RING) * 8 + lax.rem(xx, RING) * 2 + cc)

    right, left = (lax.rem(y + 1, RING), s), (lax.rem(y + 3, RING), s)
    after, before = (y, lax.rem(s + 1, 32)), (y, lax.rem(s + 31, 32))
    partner = seat(z, x, 1 - c)

    def along(axis, distance):
        return seat(z, x + distance, c) if axis == 0 else seat(z + distance, x, c)

    def w_loads(n):
        share = lax.rem(y + (2, 1, 3, 0)[n // PARTS], RING)
        columns = pl.ds(pl.multiple_of(share * SHARE + n % PARTS * PART, PART), PART)
        return [
            pltpu.make_async_copy(w_hbm.at[:, columns], w_ref.at[n, 0, z, x, c], w_sem.at[n]),
            pltpu.make_async_copy(wt_hbm.at[:, columns], w_ref.at[n, 1, z, x, c], w_sem.at[n]),
        ]

    barrier = pltpu.get_barrier_semaphore()
    steps = sorted(
        [(i, j) for i in range(RING) for j in range(RING) if i or j],
        key=lambda ij: -min(ij[0], RING - ij[0]) - min(ij[1], RING - ij[1]),
    )
    others = [seat(z + i, x + j, c) for i, j in steps]
    greeted = list(others)
    greeted += [right, left, after, before, partner]
    for device in greeted:
        pl.semaphore_signal(barrier, inc=1, device_id=device, device_id_type=MESH)

    def order(b):
        return lax.rem(b + 1, BLOCKS)

    tail = pl.ds(2 * WINDOW, 2 * TOKENS)
    kv_loads = [
        pltpu.make_async_copy(kv_hbm, raw.at[0, tail], kv_sem.at[0]),
        pltpu.make_async_copy(kvt_hbm, raw.at[1, tail], kv_sem.at[1]),
        pltpu.make_async_copy(lengths_hbm, lengths_ref, kv_sem.at[2]),
    ]

    def q_loads(k):
        here = pl.ds(pl.multiple_of(order(k) * BLOCK, BLOCK), BLOCK)
        return [
            pltpu.make_async_copy(q_hbm.at[here], q_ref.at[here], q_sem.at[k]),
            pltpu.make_async_copy(qt_hbm.at[here], qt_ref.at[here], q_sem.at[k]),
        ]

    for load in w_loads(0) + w_loads(1) + kv_loads + q_loads(0):
        load.start()
    for n in range(2, PIECES):
        for load in w_loads(n):
            load.start()
    for k in range(1, BLOCKS):
        for load in q_loads(k):
            load.start()
    def remote(src, dst, send, recv, device):
        return pltpu.make_async_remote_copy(
            src_ref=src, dst_ref=dst, send_sem=send, recv_sem=recv,
            device_id=device, device_id_type=MESH,
        )

    def one(n, half):
        piece = w_ref.at[n, half, z, x, c]
        return [
            remote(piece, piece, one_send.at[0], one_recv.at[n], along(half, d))
            for d in (2, 1, 3)
        ]

    def two(n, half):
        line = w_ref.at[n, 0, z, :, c] if half == 0 else w_ref.at[n, 1, :, x, c]
        return [
            remote(line, line, two_send.at[0], two_recv.at[n], along(1 - half, d))
            for d in (2, 1, 3)
        ]

    def core(n):
        mine = w_ref.at[n, :, :, :, c]
        return remote(mine, mine, core_send.at[0], core_recv.at[n], partner)

    def half_columns(h):
        return pl.ds(h * (PART // 2), PART // 2)

    def arrived(ref, sem):
        pltpu.make_async_copy(ref, ref, sem).wait()

    def weights_first():
        arrived(w_ref.at[0, :, 0, 0, 0], w_sem.at[0])
        for h in (0, 1):
            mine = w_ref.at[0, :, z, x, c, :, half_columns(h)]
            for device in others:
                remote(mine, mine, first_send.at[0], first_recv.at[h], device).start()

    def core_half(h):
        mine = w_ref.at[0, :, :, :, c, :, half_columns(h)]
        return remote(mine, mine, core_send.at[0], core_recv.at[h * PIECES], partner)

    def core_first(h):
        arrived(w_ref.at[pl.ds(0, 5), 0, pl.ds(0, 3), 0, :, :, half_columns(h)], first_recv.at[h])
        core_half(h).start()

    def first_ready(h):
        core_half(h).wait_recv()

    def weights_one(n):
        arrived(w_ref.at[n, :, 0, 0, 0], w_sem.at[n])
        for half in (0, 1):
            for copy in one(n, half):
                copy.start()

    def weights_two(n):
        arrived(w_ref.at[n, 0, pl.ds(0, 3), 0], one_recv.at[n])
        for half in (0, 1):
            for copy in two(n, half):
                copy.start()

    def weights_core(n):
        arrived(w_ref.at[n, 0, pl.ds(0, 3)], two_recv.at[n])
        core(n).start()

    def weights_ready(n):
        core(n).wait_recv()

    def halo(k):
        return remote(
            (kv_hbm, kvt_hbm)[k].at[pl.ds(2 * (TOKENS - WINDOW), 2 * WINDOW)],
            raw.at[k, pl.ds(0, 2 * WINDOW)], halo_sem.at[0], halo_sem.at[1], after,
        )

    pl.semaphore_wait(barrier, len(greeted))
    weights_one(1)
    weights_first()
    weights_one(2)


    def unpack(at, rows):
        for k in (0, 1):
            wide[k, : 2 * rows] = raw[k, pl.ds(2 * at, 2 * rows)].astype(jnp.float32)
            for j in (0, 1):
                ctx[j, pl.ds(at, rows), HEAD * k : HEAD * (k + 1)] = wide[
                    k, pl.ds(j, rows, stride=2), :
                ].astype(jnp.bfloat16)

    for load in kv_loads:
        load.wait()
    starts = doc_starts(lengths_ref[...])

    def unpack_step(i, carry):
        unpack(pl.multiple_of(WINDOW + i * 128, 32), 128)
        return carry

    lax.fori_loop(0, TOKENS // 128, unpack_step, 0)
    def attend_step(i):
        for k in range(TOGETHER):
            at = pl.multiple_of(lax.rem(i * STEP_ROWS + BLOCK, TOKENS) + k * STRETCH, STRETCH)
            here = pl.ds(at, STRETCH)
            span = pl.ds(at, SPAN)
            out, tan = attend_block(
                q_ref[here, :], qt_ref[here, :], ctx[0, span, :], ctx[1, span, :],
                starts, s * TOKENS + at,
            )
            for h in range(HEADS):
                rows = slice(STRETCH * h, STRETCH * (h + 1))
                aa[here, HEAD * h : HEAD * (h + 1)] = tan[rows]
                aa[here, GROUP + HEAD * h : GROUP + HEAD * (h + 1)] = out[rows]

    def project(b, n):
        here = pl.ds(pl.multiple_of(b * BLOCK, BLOCK), BLOCK)
        w = w_ref[n, 0].reshape(GROUP, PART)
        wt = w_ref[n, 1].reshape(GROUP, PART)
        att = aa[here, GROUP:]
        value = jnp.dot(att, w, preferred_element_type=jnp.float32)
        tan = jnp.dot(aa[here, :GROUP], w, preferred_element_type=jnp.float32)
        tan = tan + jnp.dot(att, wt, preferred_element_type=jnp.float32)
        return value, tan

    def d_copy(b, p, j):
        return remote(d_out.at[b, p, j], d_in.at[b, p, j], d_send.at[0], d_recv.at[b, p, j],
                      (right, left)[j])

    def m_copy(b, p, j):
        return remote(m_out.at[b, p, j], m_in.at[b, p, j], m_send.at[0], m_recv.at[b, p, j],
                      (right, left)[j])

    def far(b, p):
        value, tan = project(b, p)
        d_out[b, p, 0] = value.astype(jnp.bfloat16)
        d_out[b, p, 1] = tan.astype(jnp.bfloat16)
        d_copy(b, p, 0).start()
        d_copy(b, p, 1).start()

    def far_half(b, h):
        here = pl.ds(pl.multiple_of(b * BLOCK, BLOCK), BLOCK)
        columns = half_columns(h)
        w = w_ref[0, 0, :, :, :, :, columns].reshape(GROUP, PART // 2)
        wt = w_ref[0, 1, :, :, :, :, columns].reshape(GROUP, PART // 2)
        att = aa[here, GROUP:]
        value = jnp.dot(att, w, preferred_element_type=jnp.float32)
        tan = jnp.dot(aa[here, :GROUP], w, preferred_element_type=jnp.float32)
        tan = tan + jnp.dot(att, wt, preferred_element_type=jnp.float32)
        d_out[b, 0, 0, :, columns] = value.astype(jnp.bfloat16)
        d_out[b, 0, 1, :, columns] = tan.astype(jnp.bfloat16)
        for j in (0, 1):
            remote(
                d_out.at[b, 0, j, :, columns], d_in.at[b, 0, j, :, columns],
                d_send.at[0], d_recv.at[b, 0, j], (right, left)[j],
            ).start()

    def near(b, p, j):
        value, tan = project(b, PARTS * (1 + j) + p)
        d_copy(b, p, j).wait_recv()
        came = d_in[b, p, j].astype(jnp.float32)
        if j == 0:
            value = value + came
        else:
            tan = tan + came
        m_out[b, p, j, 0] = value.astype(jnp.bfloat16)
        m_out[b, p, j, 1] = tan.astype(jnp.bfloat16)
        m_copy(b, p, j).start()

    def home(b, p):
        value, tan = project(b, PARTS * 3 + p)
        own[b, p, 0] = value
        own[b, p, 1] = tan

    plan = {i: [] for i in range(STEPS)}

    def at(i, action, *args):
        plan[i].append((action, args))

    def far_next(k):
        far(order((0, 1, 2, 2)[k]), (1, 1, 0, 1)[k])

    def halo_start():
        halo(0).start()
        halo(1).start()

    at(1, weights_one, 3), at(1, weights_two, 1)
    at(2, core_first, 0), at(2, halo_start), at(2, weights_one, 4)
    at(3, core_first, 1)
    at(3, first_ready, 0), at(3, far_half, order(0), 0), at(3, far_half, order(1), 0)
    at(3, first_ready, 1), at(3, far_half, order(0), 1), at(3, far_half, order(1), 1)
    at(3, weights_two, 2), at(3, weights_one, 5), at(3, weights_core, 1)
    at(4, weights_ready, 1), at(4, far_next, 0), at(4, far_next, 1)
    at(4, weights_two, 3), at(4, weights_one, 6), at(4, weights_two, 4)
    at(5, far_next, 2), at(5, far_next, 3), at(5, weights_core, 2)
    at(5, weights_one, 7), at(5, weights_two, 5)
    at(6, weights_core, 3), at(6, weights_two, 6)

    def step(i, carry):
        @pl.when(i % 2 == 0)
        def _():
            arrived(aa.at[pl.ds(0, BLOCK)], q_sem.at[i // 2])

        @pl.when(i == 6)
        def _():
            arrived(raw.at[:, pl.ds(0, 2 * WINDOW)], halo_sem.at[1])
            unpack(0, WINDOW)

        attend_step(i)

        for k in range(STEPS):
            if plan[k]:
                @pl.when(i == k)
                def _():
                    for action, args in plan[k]:
                        action(*args)

        return carry

    lax.fori_loop(0, STEPS, step, 0)

    def last_far(p, carry):
        far(order(BLOCKS - 1), p)
        return carry

    lax.fori_loop(0, PARTS, last_far, 0)
    weights_two(7)
    weights_core(4)
    weights_ready(2)
    weights_ready(3)

    def near_step(k, carry):
        def right_step(p, carry):
            near(order(k), p, 0)
            return carry

        def left_step(p, carry):
            near(order(k), p, 1)
            return carry

        lax.fori_loop(0, PARTS, right_step, 0)

        @pl.when(k == 0)
        def _():
            weights_core(5)
            weights_ready(4)
            weights_ready(5)

        lax.fori_loop(0, PARTS, left_step, 0)

        @pl.when(k == 1)
        def _():
            weights_core(6)
            weights_core(7)

        return carry

    lax.fori_loop(0, BLOCKS, near_step, 0)
    weights_ready(6)
    weights_ready(7)

    def home_step(k, carry):
        home(order(k // PARTS), k % PARTS)
        return carry

    lax.fori_loop(0, BLOCKS * PARTS, home_step, 0)

    arrived(d_out, d_send.at[0])
    arrived(raw.at[:, pl.ds(0, 2 * WINDOW)], halo_sem.at[0])
    arrived(w_ref.at[pl.ds(0, 5), 0, pl.ds(0, 3), 0], first_send.at[0])
    arrived(w_ref.at[pl.ds(1, PIECES - 1), 0, pl.ds(0, 3), 0], one_send.at[0])
    arrived(w_ref.at[pl.ds(1, PIECES - 1), 0, pl.ds(0, 3)], two_send.at[0])
    arrived(w_ref.at[:, :, :, :, 0], core_send.at[0])

    def out_copy(b, p, j):
        here = pl.ds(pl.multiple_of(b * BLOCK, BLOCK), BLOCK)
        columns = pl.ds(pl.multiple_of(p * PART, PART), PART)
        return pltpu.make_async_copy(
            final.at[b, p, j], (out_ref, tan_ref)[j].at[here, columns], out_sem.at[0]
        )

    def last_step(k, carry):
        b, p = order(k // PARTS), k % PARTS
        m_copy(b, p, 0).wait_recv()
        m_copy(b, p, 1).wait_recv()
        for j in (0, 1):
            final[b, p, j] = (
                own[b, p, j]
                + m_in[b, p, 0, j].astype(jnp.float32)
                + m_in[b, p, 1, j].astype(jnp.float32)
            ).astype(jnp.bfloat16)
            out_copy(b, p, j).start()
        return carry

    lax.fori_loop(0, BLOCKS * PARTS, last_step, 0)

    arrived(m_out, m_send.at[0])
    arrived(final, out_sem.at[0])


def layer(lengths, q, qt, kv, kvt, w, wt):
    anywhere = pl.BlockSpec(memory_space=pltpu.HBM)
    shape = jax.ShapeDtypeStruct((TOKENS, SHARE), jnp.bfloat16)
    bf16, f32 = jnp.bfloat16, jnp.float32
    dma = pltpu.SemaphoreType.DMA
    return pl.pallas_call(
        layer_kernel,
        out_shape=(shape, shape),
        in_specs=[anywhere] * 7,
        out_specs=(pl.BlockSpec(memory_space=pl.ANY),) * 2,
        scratch_shapes=[
            pltpu.VMEM((1, NDOCS), jnp.int32),
            pltpu.VMEM((TOKENS, GROUP), bf16),
            pltpu.VMEM((TOKENS, GROUP), bf16),
            pltpu.VMEM((2, 2 * (WINDOW + TOKENS), HEAD), bf16),
            pltpu.VMEM((2, 2 * WINDOW, HEAD), f32),
            pltpu.VMEM((2, WINDOW + TOKENS, 2 * HEAD), bf16),
            pltpu.VMEM((PIECES, 2, RING, RING, 2, ROWS, PART), bf16),
            pltpu.VMEM((TOKENS, 2 * GROUP), bf16),
            pltpu.VMEM((BLOCKS, PARTS, 2, BLOCK, PART), bf16),
            pltpu.VMEM((BLOCKS, PARTS, 2, BLOCK, PART), bf16),
            pltpu.VMEM((BLOCKS, PARTS, 2, 2, BLOCK, PART), bf16),
            pltpu.VMEM((BLOCKS, PARTS, 2, 2, BLOCK, PART), bf16),
            pltpu.VMEM((BLOCKS, PARTS, 2, BLOCK, PART), f32),
            pltpu.VMEM((BLOCKS, PARTS, 2, BLOCK, PART), bf16),
            dma((3,)),
            dma((BLOCKS,)),
            dma((PIECES,)),
            dma((2,)),
            dma((1,)),
            dma((2,)),
            dma((1,)),
            dma((PIECES,)),
            dma((1,)),
            dma((PIECES,)),
            dma((1,)),
            dma((PIECES + 1,)),
            dma((1,)),
            dma((BLOCKS, PARTS, 2)),
            dma((1,)),
            dma((BLOCKS, PARTS, 2)),
            dma((1,)),
        ],
        compiler_params=pltpu.CompilerParams(
            collective_id=0, has_side_effects=True, vmem_limit_bytes=VMEM_LIMIT
        ),
        name="layer",
    )(lengths, q, qt, kv, kvt, w, wt)


def flush_kernel(a_ref, b_ref, a_hbm, b_hbm, sem):
    copies = [
        pltpu.make_async_copy(a_ref, a_hbm, sem.at[0]),
        pltpu.make_async_copy(b_ref, b_hbm, sem.at[1]),
    ]
    for copy in copies:
        copy.start()
    for copy in copies:
        copy.wait()


def flush(a, b):
    anywhere, hbm = pl.BlockSpec(memory_space=pl.ANY), pl.BlockSpec(memory_space=pltpu.HBM)
    shape = jax.ShapeDtypeStruct(a.shape, a.dtype)
    return pl.pallas_call(
        flush_kernel,
        out_shape=(shape, shape),
        in_specs=[anywhere, anywhere],
        out_specs=(hbm, hbm),
        scratch_shapes=[pltpu.SemaphoreType.DMA((2,))],
        compiler_params=pltpu.CompilerParams(vmem_limit_bytes=4 << 20),
        name="flush",
    )(a, b)


def body(
    queries, query_tangent, key_value, key_value_tangents, doc_lengths, out_weight, weight_tangent
):
    hold = lambda v: pltpu.with_memory_space_constraint(v, pltpu.HBM)
    rows = 2 * TOKENS
    out, tan = layer(
        hold(doc_lengths[None, :]),
        hold(queries),
        hold(query_tangent),
        hold(key_value.reshape(rows, HEAD)),
        hold(key_value_tangents.reshape(rows, HEAD)),
        hold(out_weight),
        hold(weight_tangent),
    )
    return flush(out, tan)


def solution(mesh):
    in_specs = (
        P("seq", "kv"),
        P("seq", "kv"),
        P("seq", None, "kv"),
        P("seq", None, "kv"),
        P(),
        P(("kv", "seq"), None),
        P(("kv", "seq"), None),
    )
    out_specs = (P("seq", "kv"), P("seq", "kv"))
    return jax.shard_map(body, mesh=mesh, in_specs=in_specs, out_specs=out_specs, check_vma=False)
```

```python
import functools
import math

import jax
import jax.numpy as jnp
from jax import lax
from jax.experimental import pallas as pl
from jax.experimental.pallas import tpu as pltpu
from jax.sharding import PartitionSpec as P

STRETCH = 32
WINDOW = 224
HEAD = 128
HEADS = 8
SPAN = WINDOW + STRETCH
MASKED = -1e30
SCALE = 1.0 / math.sqrt(HEAD)
EXP_SCALE = SCALE * math.log2(math.e)
MESH = pl.DeviceIdType.MESH

TOKENS = 1024
NDOCS = 256
GROUP = HEADS * HEAD
SHARE = 512
BLOCK = 256
BLOCKS = TOKENS // BLOCK
TOGETHER = 4
STEP_ROWS = TOGETHER * STRETCH
STEPS = TOKENS // STEP_ROWS
RING = 4
ROWS = 32
PART = 256
PARTS = SHARE // PART
PIECES = RING * PARTS
VMEM_LIMIT = 44 << 20


def attend_block(q, qt, keys, values, starts, position):
    rows = STRETCH * HEADS
    qs = jnp.concatenate([q[:, HEAD * h : HEAD * (h + 1)] for h in range(HEADS)], axis=0)
    qts = jnp.concatenate([qt[:, HEAD * h : HEAD * (h + 1)] for h in range(HEADS)], axis=0)
    dims = (((1,), (1,)), ((), ()))
    s = lax.dot_general(qs, keys[:, :HEAD], dims, preferred_element_type=jnp.float32)
    t = lax.dot_general(
        jnp.concatenate([qts, qs], axis=1), keys, dims, preferred_element_type=jnp.float32
    )
    row = lax.broadcasted_iota(jnp.int32, (STRETCH, SPAN), 0)
    column = lax.broadcasted_iota(jnp.int32, (STRETCH, SPAN), 1)
    here = (position + row).astype(jnp.float32)
    first = jnp.max(jnp.where(starts <= here, starts, 0.0), axis=-1, keepdims=True)
    there = (position - WINDOW + column).astype(jnp.float32)
    admitted = (there >= first) & (there <= here) & (there > here - WINDOW)
    s = jnp.where(admitted[None], s.reshape(HEADS, STRETCH, SPAN), MASKED).reshape(rows, SPAN)
    peak = jnp.max(s, axis=-1, keepdims=True)
    e = jnp.exp2((s - peak) * EXP_SCALE)
    prob = e * (1.0 / jnp.sum(e, axis=-1, keepdims=True))
    t = t * SCALE
    mean = jnp.sum(prob * t, axis=-1, keepdims=True)
    prob_t = prob * (t - mean)
    flat = (((1,), (0,)), ((), ()))
    pv = lax.dot_general(prob.astype(jnp.bfloat16), values, flat, preferred_element_type=jnp.float32)
    tv = lax.dot_general(
        prob_t.astype(jnp.bfloat16), values[:, :HEAD], flat, preferred_element_type=jnp.float32
    )
    return pv[:, :HEAD].astype(jnp.bfloat16), (tv + pv[:, HEAD:]).astype(jnp.bfloat16)


def doc_starts(lengths):
    lane = lax.broadcasted_iota(jnp.int32, (8, NDOCS), 1)
    own = jnp.broadcast_to(lengths, (8, NDOCS))
    total = own
    shift = 1
    while shift < NDOCS:
        total = total + jnp.where(lane >= shift, pltpu.roll(total, shift, 1), 0)
        shift *= 2
    return (total - own).astype(jnp.float32)[:1]


def layer_kernel(
    lengths_hbm, q_hbm, qt_hbm, kv_hbm, kvt_hbm, w_hbm, wt_hbm, out_ref, tan_ref,
    lengths_ref, q_ref, qt_ref, raw, wide, ctx, w_ref, aa, d_out, d_in, m_out, m_in, own,
    kv_sem, q_sem, w_sem, halo_sem, first_send, first_recv, one_send, one_recv, two_send, two_recv, core_send, core_recv,
    d_send, d_recv, m_send, m_recv,
):
    y = lax.axis_index("kv")
    s = lax.axis_index("seq")
    z, x, c = s // 8, (s // 2) % RING, s % 2

    def seat(zz, xx, cc):
        return (y, lax.rem(zz, RING) * 8 + lax.rem(xx, RING) * 2 + cc)

    right, left = (lax.rem(y + 1, RING), s), (lax.rem(y + 3, RING), s)
    after, before = (y, lax.rem(s + 1, 32)), (y, lax.rem(s + 31, 32))
    partner = seat(z, x, 1 - c)

    def along(axis, distance):
        return seat(z, x + distance, c) if axis == 0 else seat(z + distance, x, c)

    def w_loads(n):
        share = lax.rem(y + (2, 1, 3, 0)[n // PARTS], RING)
        columns = pl.ds(pl.multiple_of(share * SHARE + n % PARTS * PART, PART), PART)
        return [
            pltpu.make_async_copy(w_hbm.at[:, columns], w_ref.at[n, 0, z, x, c], w_sem.at[n]),
            pltpu.make_async_copy(wt_hbm.at[:, columns], w_ref.at[n, 1, z, x, c], w_sem.at[n]),
        ]

    barrier = pltpu.get_barrier_semaphore()
    steps = sorted(
        [(i, j) for i in range(RING) for j in range(RING) if i or j],
        key=lambda ij: -min(ij[0], RING - ij[0]) - min(ij[1], RING - ij[1]),
    )
    others = [seat(z + i, x + j, c) for i, j in steps]
    greeted = list(others)
    greeted += [right, left, after, before, partner]
    for device in greeted:
        pl.semaphore_signal(barrier, inc=1, device_id=device, device_id_type=MESH)

    def order(b):
        return lax.rem(b + 1, BLOCKS)

    tail = pl.ds(2 * WINDOW, 2 * TOKENS)
    kv_loads = [
        pltpu.make_async_copy(kv_hbm, raw.at[0, tail], kv_sem.at[0]),
        pltpu.make_async_copy(kvt_hbm, raw.at[1, tail], kv_sem.at[1]),
        pltpu.make_async_copy(lengths_hbm, lengths_ref, kv_sem.at[2]),
    ]

    def q_loads(k):
        here = pl.ds(pl.multiple_of(order(k) * BLOCK, BLOCK), BLOCK)
        return [
            pltpu.make_async_copy(q_hbm.at[here], q_ref.at[here], q_sem.at[k]),
            pltpu.make_async_copy(qt_hbm.at[here], qt_ref.at[here], q_sem.at[k]),
        ]

    for load in w_loads(0) + w_loads(1) + kv_loads + q_loads(0):
        load.start()
    for n in range(2, PIECES):
        for load in w_loads(n):
            load.start()
    for k in range(1, BLOCKS):
        for load in q_loads(k):
            load.start()
    def remote(src, dst, send, recv, device):
        return pltpu.make_async_remote_copy(
            src_ref=src, dst_ref=dst, send_sem=send, recv_sem=recv,
            device_id=device, device_id_type=MESH,
        )

    def one(n, half):
        piece = w_ref.at[n, half, z, x, c]
        return [
            remote(piece, piece, one_send.at[0], one_recv.at[n], along(half, d))
            for d in (2, 1, 3)
        ]

    def two(n, half):
        line = w_ref.at[n, 0, z, :, c] if half == 0 else w_ref.at[n, 1, :, x, c]
        return [
            remote(line, line, two_send.at[0], two_recv.at[n], along(1 - half, d))
            for d in (2, 1, 3)
        ]

    def core(n):
        mine = w_ref.at[n, :, :, :, c]
        return remote(mine, mine, core_send.at[0], core_recv.at[n], partner)

    def half_columns(h):
        return pl.ds(h * (PART // 2), PART // 2)

    def arrived(ref, sem):
        pltpu.make_async_copy(ref, ref, sem).wait()

    def weights_first():
        arrived(w_ref.at[0, :, 0, 0, 0], w_sem.at[0])
        for h in (0, 1):
            mine = w_ref.at[0, :, z, x, c, :, half_columns(h)]
            for device in others:
                remote(mine, mine, first_send.at[0], first_recv.at[h], device).start()
            if h == 0:
                weights_one(1)

    def core_half(h):
        mine = w_ref.at[0, :, :, :, c, :, half_columns(h)]
        return remote(mine, mine, core_send.at[0], core_recv.at[h * PIECES], partner)

    def core_first(h):
        arrived(w_ref.at[pl.ds(0, 5), 0, pl.ds(0, 3), 0, :, :, half_columns(h)], first_recv.at[h])
        core_half(h).start()

    def first_ready(h):
        core_half(h).wait_recv()

    def weights_one(n):
        arrived(w_ref.at[n, :, 0, 0, 0], w_sem.at[n])
        for half in (0, 1):
            for copy in one(n, half):
                copy.start()

    def weights_two(n):
        arrived(w_ref.at[n, 0, pl.ds(0, 3), 0], one_recv.at[n])
        for half in (0, 1):
            for copy in two(n, half):
                copy.start()

    def weights_core(n):
        arrived(w_ref.at[n, 0, pl.ds(0, 3)], two_recv.at[n])
        core(n).start()

    def weights_ready(n):
        core(n).wait_recv()

    def halo(k):
        return remote(
            (kv_hbm, kvt_hbm)[k].at[pl.ds(2 * (TOKENS - WINDOW), 2 * WINDOW)],
            raw.at[k, pl.ds(0, 2 * WINDOW)], halo_sem.at[0], halo_sem.at[1], after,
        )

    pl.semaphore_wait(barrier, len(greeted))
    weights_first()
    weights_one(2)


    def unpack(at, rows):
        for k in (0, 1):
            wide[k, : 2 * rows] = raw[k, pl.ds(2 * at, 2 * rows)].astype(jnp.float32)
            for j in (0, 1):
                ctx[j, pl.ds(at, rows), HEAD * k : HEAD * (k + 1)] = wide[
                    k, pl.ds(j, rows, stride=2), :
                ].astype(jnp.bfloat16)

    for load in kv_loads:
        load.wait()
    starts = doc_starts(lengths_ref[...])

    def unpack_step(i, carry):
        unpack(pl.multiple_of(WINDOW + i * 128, 32), 128)
        return carry

    lax.fori_loop(0, TOKENS // 128, unpack_step, 0)
    def attend_step(i, start=0, count=TOGETHER):
        for k in range(count):
            at = lax.rem(i * STEP_ROWS + BLOCK, TOKENS) + (start + k) * STRETCH
            at = pl.multiple_of(at, STRETCH)
            here = pl.ds(at, STRETCH)
            span = pl.ds(at, SPAN)
            out, tan = attend_block(
                q_ref[here, :], qt_ref[here, :], ctx[0, span, :], ctx[1, span, :],
                starts, s * TOKENS + at,
            )
            for h in range(HEADS):
                rows = slice(STRETCH * h, STRETCH * (h + 1))
                aa[here, HEAD * h : HEAD * (h + 1)] = tan[rows]
                aa[here, GROUP + HEAD * h : GROUP + HEAD * (h + 1)] = out[rows]

    def project(b, n):
        here = pl.ds(pl.multiple_of(b * BLOCK, BLOCK), BLOCK)
        w = w_ref[n, 0].reshape(GROUP, PART)
        wt = w_ref[n, 1].reshape(GROUP, PART)
        att = aa[here, GROUP:]
        value = jnp.dot(att, w, preferred_element_type=jnp.float32)
        tan = jnp.dot(aa[here, :GROUP], w, preferred_element_type=jnp.float32)
        tan = tan + jnp.dot(att, wt, preferred_element_type=jnp.float32)
        return value, tan

    def d_copy(b, p, j):
        return remote(d_out.at[b, p, j], d_in.at[b, p, j], d_send.at[0], d_recv.at[b, p, j],
                      (right, left)[j])

    def m_copy(b, p, j):
        return remote(m_out.at[b, p, j], m_in.at[b, p, j], m_send.at[0], m_recv.at[b, p],
                      (right, left)[j])

    def far(b, p):
        value, tan = project(b, p)
        d_out[b, p, 0] = value.astype(jnp.bfloat16)
        d_out[b, p, 1] = tan.astype(jnp.bfloat16)
        d_copy(b, p, 0).start()
        d_copy(b, p, 1).start()

    def far_half(b, h):
        here = pl.ds(pl.multiple_of(b * BLOCK, BLOCK), BLOCK)
        columns = half_columns(h)
        w = w_ref[0, 0, :, :, :, :, columns].reshape(GROUP, PART // 2)
        wt = w_ref[0, 1, :, :, :, :, columns].reshape(GROUP, PART // 2)
        att = aa[here, GROUP:]
        value = jnp.dot(att, w, preferred_element_type=jnp.float32)
        tan = jnp.dot(aa[here, :GROUP], w, preferred_element_type=jnp.float32)
        tan = tan + jnp.dot(att, wt, preferred_element_type=jnp.float32)
        d_out[b, 0, 0, :, columns] = value.astype(jnp.bfloat16)
        d_out[b, 0, 1, :, columns] = tan.astype(jnp.bfloat16)
        for j in (0, 1):
            remote(
                d_out.at[b, 0, j, :, columns], d_in.at[b, 0, j, :, columns],
                d_send.at[0], d_recv.at[b, 0, j], (right, left)[j],
            ).start()

    def near(b, p, j):
        value, tan = project(b, PARTS * (1 + j) + p)
        d_copy(b, p, j).wait_recv()
        came = d_in[b, p, j].astype(jnp.float32)
        if j == 0:
            value = value + came
        else:
            tan = tan + came
        m_out[b, p, j, 0] = value.astype(jnp.bfloat16)
        m_out[b, p, j, 1] = tan.astype(jnp.bfloat16)
        m_copy(b, p, j).start()

    def home(b, p):
        value, tan = project(b, PARTS * 3 + p)
        own[b, p, 0] = value
        own[b, p, 1] = tan

    plan = {i: [] for i in range(STEPS)}

    def at(i, action, *args):
        plan[i].append((action, args))

    def far_next(k):
        far(order((0, 1, 2, 2)[k]), (1, 1, 0, 1)[k])

    def halo_start():
        halo(0).start()
        halo(1).start()

    at(2, core_first, 0), at(2, weights_one, 3), at(2, weights_two, 1)
    at(2, halo_start), at(2, weights_one, 4)
    at(3, core_first, 1), at(3, far_half, order(1), 0)
    at(3, first_ready, 1), at(3, far_half, order(0), 1), at(3, far_half, order(1), 1)
    at(3, weights_two, 2), at(3, weights_one, 5), at(3, weights_core, 1)
    at(4, weights_ready, 1), at(4, far_next, 0), at(4, far_next, 1)
    at(4, weights_two, 3), at(4, weights_one, 6), at(4, weights_two, 4)
    at(5, far_next, 2), at(5, far_next, 3), at(5, weights_core, 2)
    at(5, weights_one, 7), at(5, weights_two, 5)
    at(6, weights_core, 3), at(6, weights_two, 6)

    def step(i, carry):
        @pl.when(i % 2 == 0)
        def _():
            arrived(aa.at[pl.ds(0, BLOCK)], q_sem.at[i // 2])

        @pl.when(i == 6)
        def _():
            arrived(raw.at[:, pl.ds(0, 2 * WINDOW)], halo_sem.at[1])
            unpack(0, WINDOW)

        @pl.when(i != 3)
        def _():
            attend_step(i)

        @pl.when(i == 3)
        def _():
            def half_step(k, carry):
                attend_step(3, 2 * k, 2)

                @pl.when(k == 0)
                def _():
                    first_ready(0)
                    far_half(order(0), 0)

                return carry

            lax.fori_loop(0, 2, half_step, 0)

        for k in range(STEPS):
            if plan[k]:
                @pl.when(i == k)
                def _():
                    for action, args in plan[k]:
                        action(*args)

        return carry

    lax.fori_loop(0, STEPS, step, 0)

    def last_far(p, carry):
        far(order(BLOCKS - 1), p)
        return carry

    lax.fori_loop(0, PARTS, last_far, 0)
    weights_two(7)
    weights_core(4)
    weights_ready(2)
    weights_ready(3)

    def near_step(k, carry):
        def right_step(p, carry):
            near(order(k), p, 0)
            return carry

        def left_step(p, carry):
            near(order(k), p, 1)
            return carry

        lax.fori_loop(0, PARTS, right_step, 0)

        @pl.when(k == 0)
        def _():
            weights_core(5)
            weights_ready(4)
            weights_ready(5)

        lax.fori_loop(0, PARTS, left_step, 0)

        @pl.when(k == 1)
        def _():
            weights_core(6)
            weights_core(7)

        return carry

    lax.fori_loop(0, BLOCKS, near_step, 0)
    weights_ready(6)
    weights_ready(7)

    def home_step(k, carry):
        home(order(k // PARTS), k % PARTS)
        return carry

    lax.fori_loop(0, BLOCKS * PARTS, home_step, 0)

    arrived(d_out, d_send.at[0])
    arrived(raw.at[:, pl.ds(0, 2 * WINDOW)], halo_sem.at[0])
    arrived(w_ref.at[pl.ds(0, 5), 0, pl.ds(0, 3), 0], first_send.at[0])
    arrived(w_ref.at[pl.ds(1, PIECES - 1), 0, pl.ds(0, 3), 0], one_send.at[0])
    arrived(w_ref.at[pl.ds(1, PIECES - 1), 0, pl.ds(0, 3)], two_send.at[0])
    arrived(w_ref.at[:, :, :, :, 0], core_send.at[0])

    def last_step(k, carry):
        b, p = order(k // PARTS), k % PARTS
        arrived(m_in.at[b, p], m_recv.at[b, p])
        here = pl.ds(pl.multiple_of(b * BLOCK, BLOCK), BLOCK)
        columns = pl.ds(pl.multiple_of(p * PART, PART), PART)
        for j, ref in ((0, out_ref), (1, tan_ref)):
            ref[here, columns] = (
                own[b, p, j]
                + m_in[b, p, 0, j].astype(jnp.float32)
                + m_in[b, p, 1, j].astype(jnp.float32)
            ).astype(jnp.bfloat16)
        return carry

    lax.fori_loop(0, BLOCKS * PARTS, last_step, 0)

    arrived(m_out, m_send.at[0])


def layer(lengths, q, qt, kv, kvt, w, wt):
    anywhere = pl.BlockSpec(memory_space=pltpu.HBM)
    shape = jax.ShapeDtypeStruct((TOKENS, SHARE), jnp.bfloat16)
    bf16, f32 = jnp.bfloat16, jnp.float32
    dma = pltpu.SemaphoreType.DMA
    return pl.pallas_call(
        layer_kernel,
        out_shape=(shape, shape),
        in_specs=[anywhere] * 7,
        out_specs=(pl.BlockSpec(memory_space=pltpu.VMEM),) * 2,
        scratch_shapes=[
            pltpu.VMEM((1, NDOCS), jnp.int32),
            pltpu.VMEM((TOKENS, GROUP), bf16),
            pltpu.VMEM((TOKENS, GROUP), bf16),
            pltpu.VMEM((2, 2 * (WINDOW + TOKENS), HEAD), bf16),
            pltpu.VMEM((2, 2 * WINDOW, HEAD), f32),
            pltpu.VMEM((2, WINDOW + TOKENS, 2 * HEAD), bf16),
            pltpu.VMEM((PIECES, 2, RING, RING, 2, ROWS, PART), bf16),
            pltpu.VMEM((TOKENS, 2 * GROUP), bf16),
            pltpu.VMEM((BLOCKS, PARTS, 2, BLOCK, PART), bf16),
            pltpu.VMEM((BLOCKS, PARTS, 2, BLOCK, PART), bf16),
            pltpu.VMEM((BLOCKS, PARTS, 2, 2, BLOCK, PART), bf16),
            pltpu.VMEM((BLOCKS, PARTS, 2, 2, BLOCK, PART), bf16),
            pltpu.VMEM((BLOCKS, PARTS, 2, BLOCK, PART), f32),
            dma((3,)),
            dma((BLOCKS,)),
            dma((PIECES,)),
            dma((2,)),
            dma((1,)),
            dma((2,)),
            dma((1,)),
            dma((PIECES,)),
            dma((1,)),
            dma((PIECES,)),
            dma((1,)),
            dma((PIECES + 1,)),
            dma((1,)),
            dma((BLOCKS, PARTS, 2)),
            dma((1,)),
            dma((BLOCKS, PARTS)),
        ],
        compiler_params=pltpu.CompilerParams(
            collective_id=0, has_side_effects=True, vmem_limit_bytes=VMEM_LIMIT
        ),
        name="layer",
    )(lengths, q, qt, kv, kvt, w, wt)


def flush_kernel(a_ref, b_ref, a_hbm, b_hbm, sem):
    copies = [
        pltpu.make_async_copy(a_ref, a_hbm, sem.at[0]),
        pltpu.make_async_copy(b_ref, b_hbm, sem.at[1]),
    ]
    for copy in copies:
        copy.start()
    for copy in copies:
        copy.wait()


def flush(a, b):
    anywhere, hbm = pl.BlockSpec(memory_space=pl.ANY), pl.BlockSpec(memory_space=pltpu.HBM)
    shape = jax.ShapeDtypeStruct(a.shape, a.dtype)
    return pl.pallas_call(
        flush_kernel,
        out_shape=(shape, shape),
        in_specs=[anywhere, anywhere],
        out_specs=(hbm, hbm),
        scratch_shapes=[pltpu.SemaphoreType.DMA((2,))],
        compiler_params=pltpu.CompilerParams(vmem_limit_bytes=4 << 20),
        name="flush",
    )(a, b)


def body(
    queries, query_tangent, key_value, key_value_tangents, doc_lengths, out_weight, weight_tangent
):
    hold = lambda v: pltpu.with_memory_space_constraint(v, pltpu.HBM)
    rows = 2 * TOKENS
    out, tan = layer(
        hold(doc_lengths[None, :]),
        hold(queries),
        hold(query_tangent),
        hold(key_value.reshape(rows, HEAD)),
        hold(key_value_tangents.reshape(rows, HEAD)),
        hold(out_weight),
        hold(weight_tangent),
    )
    return flush(out, tan)


def solution(mesh):
    in_specs = (
        P("seq", "kv"),
        P("seq", "kv"),
        P("seq", None, "kv"),
        P("seq", None, "kv"),
        P(),
        P(("kv", "seq"), None),
        P(("kv", "seq"), None),
    )
    out_specs = (P("seq", "kv"), P("seq", "kv"))
    return jax.shard_map(body, mesh=mesh, in_specs=in_specs, out_specs=out_specs, check_vma=False)
```

```python
import functools
import math

import jax
import jax.numpy as jnp
from jax import lax
from jax.experimental import pallas as pl
from jax.experimental.pallas import tpu as pltpu
from jax.sharding import PartitionSpec as P

STRETCH = 32
WINDOW = 224
HEAD = 128
HEADS = 8
SPAN = WINDOW + STRETCH
MASKED = -1e30
SCALE = 1.0 / math.sqrt(HEAD)
EXP_SCALE = SCALE * math.log2(math.e)
MESH = pl.DeviceIdType.MESH

TOKENS = 1024
NDOCS = 256
GROUP = HEADS * HEAD
SHARE = 512
BLOCK = 256
BLOCKS = TOKENS // BLOCK
TOGETHER = 4
STEP_ROWS = TOGETHER * STRETCH
STEPS = TOKENS // STEP_ROWS
RING = 4
ROWS = 32
PART = 256
PARTS = SHARE // PART
PIECES = RING * PARTS
VMEM_LIMIT = 44 << 20


def attend_block(q, qt, keys, values, starts, position):
    rows = STRETCH * HEADS
    qs = jnp.concatenate([q[:, HEAD * h : HEAD * (h + 1)] for h in range(HEADS)], axis=0)
    qts = jnp.concatenate([qt[:, HEAD * h : HEAD * (h + 1)] for h in range(HEADS)], axis=0)
    dims = (((1,), (1,)), ((), ()))
    s = lax.dot_general(qs, keys[:, :HEAD], dims, preferred_element_type=jnp.float32)
    t = lax.dot_general(
        jnp.concatenate([qts, qs], axis=1), keys, dims, preferred_element_type=jnp.float32
    )
    row = lax.broadcasted_iota(jnp.int32, (STRETCH, SPAN), 0)
    column = lax.broadcasted_iota(jnp.int32, (STRETCH, SPAN), 1)
    here = (position + row).astype(jnp.float32)
    first = jnp.max(jnp.where(starts <= here, starts, 0.0), axis=-1, keepdims=True)
    there = (position - WINDOW + column).astype(jnp.float32)
    admitted = (there >= first) & (there <= here) & (there > here - WINDOW)
    s = jnp.where(admitted[None], s.reshape(HEADS, STRETCH, SPAN), MASKED).reshape(rows, SPAN)
    peak = jnp.max(s, axis=-1, keepdims=True)
    e = jnp.exp2((s - peak) * EXP_SCALE)
    prob = e * (1.0 / jnp.sum(e, axis=-1, keepdims=True))
    t = t * SCALE
    mean = jnp.sum(prob * t, axis=-1, keepdims=True)
    prob_t = prob * (t - mean)
    flat = (((1,), (0,)), ((), ()))
    pv = lax.dot_general(prob.astype(jnp.bfloat16), values, flat, preferred_element_type=jnp.float32)
    tv = lax.dot_general(
        prob_t.astype(jnp.bfloat16), values[:, :HEAD], flat, preferred_element_type=jnp.float32
    )
    return pv[:, :HEAD].astype(jnp.bfloat16), (tv + pv[:, HEAD:]).astype(jnp.bfloat16)


def doc_starts(lengths):
    lane = lax.broadcasted_iota(jnp.int32, (8, NDOCS), 1)
    own = jnp.broadcast_to(lengths, (8, NDOCS))
    total = own
    shift = 1
    while shift < NDOCS:
        total = total + jnp.where(lane >= shift, pltpu.roll(total, shift, 1), 0)
        shift *= 2
    return (total - own).astype(jnp.float32)[:1]


def layer_kernel(
    lengths_hbm, q_hbm, qt_hbm, kv_hbm, kvt_hbm, w_hbm, wt_hbm, out_ref, tan_ref,
    lengths_ref, q_ref, qt_ref, raw, wide, ctx, w_ref, aa, d_out, d_in, m_out, m_in, own,
    kv_sem, q_sem, w_sem, halo_sem, first_send, first_recv, one_send, one_recv, two_send, two_recv, core_send, core_recv,
    d_send, d_recv, m_send, m_recv,
):
    y = lax.axis_index("kv")
    s = lax.axis_index("seq")
    z, x, c = s // 8, (s // 2) % RING, s % 2

    def seat(zz, xx, cc):
        return (y, lax.rem(zz, RING) * 8 + lax.rem(xx, RING) * 2 + cc)

    right, left = (lax.rem(y + 1, RING), s), (lax.rem(y + 3, RING), s)
    after, before = (y, lax.rem(s + 1, 32)), (y, lax.rem(s + 31, 32))
    partner = seat(z, x, 1 - c)

    def along(axis, distance):
        return seat(z, x + distance, c) if axis == 0 else seat(z + distance, x, c)

    def w_loads(n):
        share = lax.rem(y + (2, 1, 3, 0)[n // PARTS], RING)
        columns = pl.ds(pl.multiple_of(share * SHARE + n % PARTS * PART, PART), PART)
        return [
            pltpu.make_async_copy(w_hbm.at[:, columns], w_ref.at[n, 0, z, x, c], w_sem.at[min(n, 1)]),
            pltpu.make_async_copy(wt_hbm.at[:, columns], w_ref.at[n, 1, z, x, c], w_sem.at[min(n, 1)]),
        ]

    barrier = pltpu.get_barrier_semaphore()
    steps = sorted(
        [(i, j) for i in range(RING) for j in range(RING) if i or j],
        key=lambda ij: -min(ij[0], RING - ij[0]) - min(ij[1], RING - ij[1]),
    )
    others = [seat(z + i, x + j, c) for i, j in steps]
    greeted = list(others)
    greeted += [right, left, after, before, partner]
    for device in greeted:
        pl.semaphore_signal(barrier, inc=1, device_id=device, device_id_type=MESH)

    def order(b):
        return lax.rem(b + 1, BLOCKS)

    tail = pl.ds(2 * WINDOW, 2 * TOKENS)
    kv_loads = [
        pltpu.make_async_copy(kv_hbm, raw.at[0, tail], kv_sem.at[0]),
        pltpu.make_async_copy(kvt_hbm, raw.at[1, tail], kv_sem.at[1]),
        pltpu.make_async_copy(lengths_hbm, lengths_ref, kv_sem.at[2]),
    ]

    def q_loads(k):
        here = pl.ds(pl.multiple_of(order(k) * BLOCK, BLOCK), BLOCK)
        return [
            pltpu.make_async_copy(q_hbm.at[here], q_ref.at[here], q_sem.at[k]),
            pltpu.make_async_copy(qt_hbm.at[here], qt_ref.at[here], q_sem.at[k]),
        ]

    for load in w_loads(0) + w_loads(1) + kv_loads + q_loads(0):
        load.start()
    for n in range(2, PIECES):
        for load in w_loads(n):
            load.start()
    for k in range(1, BLOCKS):
        for load in q_loads(k):
            load.start()
    def remote(src, dst, send, recv, device):
        return pltpu.make_async_remote_copy(
            src_ref=src, dst_ref=dst, send_sem=send, recv_sem=recv,
            device_id=device, device_id_type=MESH,
        )

    def one(n, half):
        piece = w_ref.at[n, half, z, x, c]
        return [
            remote(piece, piece, one_send.at[0], one_recv.at[n], along(half, d))
            for d in (2, 1, 3)
        ]

    def two(n, half):
        line = w_ref.at[n, 0, z, :, c] if half == 0 else w_ref.at[n, 1, :, x, c]
        return [
            remote(line, line, two_send.at[0], two_recv.at[n], along(1 - half, d))
            for d in (2, 1, 3)
        ]

    def core(n):
        mine = w_ref.at[n, :, :, :, c]
        return remote(mine, mine, core_send.at[0], core_recv.at[n], partner)

    def half_columns(h):
        return pl.ds(h * (PART // 2), PART // 2)

    def arrived(ref, sem):
        pltpu.make_async_copy(ref, ref, sem).wait()

    def weights_first():
        arrived(w_ref.at[0, :, 0, 0, 0], w_sem.at[0])
        for h in (0, 1):
            mine = w_ref.at[0, :, z, x, c, :, half_columns(h)]
            for device in others:
                remote(mine, mine, first_send.at[0], first_recv.at[h], device).start()
            if h == 0:
                weights_one(1)

    def core_half(h):
        mine = w_ref.at[0, :, :, :, c, :, half_columns(h)]
        return remote(mine, mine, core_send.at[0], core_recv.at[h * PIECES], partner)

    def core_first(h):
        arrived(w_ref.at[pl.ds(0, 5), 0, pl.ds(0, 3), 0, :, :, half_columns(h)], first_recv.at[h])
        core_half(h).start()

    def first_ready(h):
        core_half(h).wait_recv()

    def weights_one(n):
        if n == 1:
            arrived(w_ref.at[pl.ds(1, PIECES - 1), :, 0, 0, 0], w_sem.at[1])
        for half in (0, 1):
            for copy in one(n, half):
                copy.start()

    def weights_two(n):
        arrived(w_ref.at[n, 0, pl.ds(0, 3), 0], one_recv.at[n])
        for half in (0, 1):
            for copy in two(n, half):
                copy.start()

    def weights_core(n):
        arrived(w_ref.at[n, 0, pl.ds(0, 3)], two_recv.at[n])
        core(n).start()

    def weights_ready(n):
        core(n).wait_recv()

    def halo(k):
        return remote(
            (kv_hbm, kvt_hbm)[k].at[pl.ds(2 * (TOKENS - WINDOW), 2 * WINDOW)],
            raw.at[k, pl.ds(0, 2 * WINDOW)], halo_sem.at[0], halo_sem.at[1], after,
        )

    pl.semaphore_wait(barrier, len(greeted))
    weights_first()
    weights_one(2)


    def unpack(at, rows):
        for k in (0, 1):
            wide[k, : 2 * rows] = raw[k, pl.ds(2 * at, 2 * rows)].astype(jnp.float32)
            for j in (0, 1):
                ctx[j, pl.ds(at, rows), HEAD * k : HEAD * (k + 1)] = wide[
                    k, pl.ds(j, rows, stride=2), :
                ].astype(jnp.bfloat16)

    for load in kv_loads:
        load.wait()
    starts = doc_starts(lengths_ref[...])

    def unpack_step(i, carry):
        unpack(pl.multiple_of(WINDOW + i * 128, 32), 128)
        return carry

    lax.fori_loop(0, TOKENS // 128, unpack_step, 0)
    def attend_step(i, start=0, count=TOGETHER):
        for k in range(count):
            at = lax.rem(i * STEP_ROWS + BLOCK, TOKENS) + (start + k) * STRETCH
            at = pl.multiple_of(at, STRETCH)
            here = pl.ds(at, STRETCH)
            span = pl.ds(at, SPAN)
            out, tan = attend_block(
                q_ref[here, :], qt_ref[here, :], ctx[0, span, :], ctx[1, span, :],
                starts, s * TOKENS + at,
            )
            for h in range(HEADS):
                rows = slice(STRETCH * h, STRETCH * (h + 1))
                aa[here, HEAD * h : HEAD * (h + 1)] = tan[rows]
                aa[here, GROUP + HEAD * h : GROUP + HEAD * (h + 1)] = out[rows]

    def project(b, n):
        here = pl.ds(pl.multiple_of(b * BLOCK, BLOCK), BLOCK)
        w = w_ref[n, 0].reshape(GROUP, PART)
        wt = w_ref[n, 1].reshape(GROUP, PART)
        att = aa[here, GROUP:]
        value = jnp.dot(att, w, preferred_element_type=jnp.float32)
        tan = jnp.dot(aa[here, :GROUP], w, preferred_element_type=jnp.float32)
        tan = tan + jnp.dot(att, wt, preferred_element_type=jnp.float32)
        return value, tan

    def d_copy(b, p, j):
        return remote(d_out.at[b, p, j], d_in.at[b, p, j], d_send.at[0], d_recv.at[b, j],
                      (right, left)[j])

    def m_copy(b, p, j):
        return remote(m_out.at[b, p, j], m_in.at[b, p, j], m_send.at[0], m_recv.at[b, p],
                      (right, left)[j])

    def far(b, p):
        value, tan = project(b, p)
        d_out[b, p, 0] = value.astype(jnp.bfloat16)
        d_out[b, p, 1] = tan.astype(jnp.bfloat16)
        d_copy(b, p, 0).start()
        d_copy(b, p, 1).start()

    def far_half(b, h):
        here = pl.ds(pl.multiple_of(b * BLOCK, BLOCK), BLOCK)
        columns = half_columns(h)
        w = w_ref[0, 0, :, :, :, :, columns].reshape(GROUP, PART // 2)
        wt = w_ref[0, 1, :, :, :, :, columns].reshape(GROUP, PART // 2)
        att = aa[here, GROUP:]
        value = jnp.dot(att, w, preferred_element_type=jnp.float32)
        tan = jnp.dot(aa[here, :GROUP], w, preferred_element_type=jnp.float32)
        tan = tan + jnp.dot(att, wt, preferred_element_type=jnp.float32)
        d_out[b, 0, 0, :, columns] = value.astype(jnp.bfloat16)
        d_out[b, 0, 1, :, columns] = tan.astype(jnp.bfloat16)
        for j in (0, 1):
            remote(
                d_out.at[b, 0, j, :, columns], d_in.at[b, 0, j, :, columns],
                d_send.at[0], d_recv.at[b, j], (right, left)[j],
            ).start()

    def near(b, p, j):
        value, tan = project(b, PARTS * (1 + j) + p)
        came = d_in[b, p, j].astype(jnp.float32)
        if j == 0:
            value = value + came
        else:
            tan = tan + came
        m_out[b, p, j, 0] = value.astype(jnp.bfloat16)
        m_out[b, p, j, 1] = tan.astype(jnp.bfloat16)
        m_copy(b, p, j).start()

    def home(b, p):
        value, tan = project(b, PARTS * 3 + p)
        own[b, p, 0] = value
        own[b, p, 1] = tan

    plan = {i: [] for i in range(STEPS)}

    def at(i, action, *args):
        plan[i].append((action, args))

    def far_next(k):
        far(order((0, 1, 2, 2)[k]), (1, 1, 0, 1)[k])

    def halo_start():
        halo(0).start()
        halo(1).start()

    at(2, core_first, 0), at(2, weights_one, 3), at(2, weights_two, 1)
    at(2, halo_start), at(2, weights_one, 4)
    at(3, core_first, 1), at(3, far_half, order(1), 0)
    at(3, first_ready, 1), at(3, far_half, order(0), 1), at(3, far_half, order(1), 1)
    at(3, weights_two, 2), at(3, weights_one, 5), at(3, weights_core, 1)
    at(4, weights_ready, 1), at(4, far_next, 0), at(4, far_next, 1)
    at(4, weights_two, 3), at(4, weights_one, 6), at(4, weights_two, 4)
    at(5, far_next, 2), at(5, far_next, 3), at(5, weights_core, 2)
    at(5, weights_one, 7), at(5, weights_two, 5)
    at(6, weights_core, 3), at(6, weights_two, 6)

    def step(i, carry):
        @pl.when(i % 2 == 0)
        def _():
            arrived(aa.at[pl.ds(0, BLOCK)], q_sem.at[i // 2])

        @pl.when(i == 6)
        def _():
            arrived(raw.at[:, pl.ds(0, 2 * WINDOW)], halo_sem.at[1])
            unpack(0, WINDOW)

        @pl.when(i != 3)
        def _():
            attend_step(i)

        @pl.when(i == 3)
        def _():
            def half_step(k, carry):
                attend_step(3, 2 * k, 2)

                @pl.when(k == 0)
                def _():
                    first_ready(0)
                    far_half(order(0), 0)

                return carry

            lax.fori_loop(0, 2, half_step, 0)

        for k in range(STEPS):
            if plan[k]:
                @pl.when(i == k)
                def _():
                    for action, args in plan[k]:
                        action(*args)

        return carry

    lax.fori_loop(0, STEPS, step, 0)

    def last_far(p, carry):
        far(order(BLOCKS - 1), p)
        return carry

    lax.fori_loop(0, PARTS, last_far, 0)
    weights_two(7)
    weights_core(4)
    weights_ready(2)
    weights_ready(3)

    def near_step(k, carry):
        def right_step(p, carry):
            near(order(k), p, 0)
            return carry

        def left_step(p, carry):
            near(order(k), p, 1)
            return carry

        arrived(d_in.at[order(k), :, 0], d_recv.at[order(k), 0])
        lax.fori_loop(0, PARTS, right_step, 0)

        @pl.when(k == 0)
        def _():
            weights_core(5)
            weights_ready(4)
            weights_ready(5)

        arrived(d_in.at[order(k), :, 1], d_recv.at[order(k), 1])
        lax.fori_loop(0, PARTS, left_step, 0)

        @pl.when(k == 1)
        def _():
            weights_core(6)
            weights_core(7)

        return carry

    lax.fori_loop(0, BLOCKS, near_step, 0)
    weights_ready(6)
    weights_ready(7)

    def home_step(k, carry):
        home(order(k // PARTS), k % PARTS)
        return carry

    lax.fori_loop(0, BLOCKS * PARTS, home_step, 0)

    arrived(d_out, d_send.at[0])
    arrived(raw.at[:, pl.ds(0, 2 * WINDOW)], halo_sem.at[0])
    arrived(w_ref.at[pl.ds(0, 5), 0, pl.ds(0, 3), 0], first_send.at[0])
    arrived(w_ref.at[pl.ds(1, PIECES - 1), 0, pl.ds(0, 3), 0], one_send.at[0])
    arrived(w_ref.at[pl.ds(1, PIECES - 1), 0, pl.ds(0, 3)], two_send.at[0])
    arrived(w_ref.at[:, :, :, :, 0], core_send.at[0])

    def last_step(k, carry):
        b, p = order(k // PARTS), k % PARTS
        arrived(m_in.at[b, p], m_recv.at[b, p])
        here = pl.ds(pl.multiple_of(b * BLOCK, BLOCK), BLOCK)
        columns = pl.ds(pl.multiple_of(p * PART, PART), PART)
        for j, ref in ((0, out_ref), (1, tan_ref)):
            ref[here, columns] = (
                own[b, p, j]
                + m_in[b, p, 0, j].astype(jnp.float32)
                + m_in[b, p, 1, j].astype(jnp.float32)
            ).astype(jnp.bfloat16)
        return carry

    lax.fori_loop(0, BLOCKS * PARTS, last_step, 0)

    arrived(m_out, m_send.at[0])


def layer(lengths, q, qt, kv, kvt, w, wt):
    anywhere = pl.BlockSpec(memory_space=pltpu.HBM)
    shape = jax.ShapeDtypeStruct((TOKENS, SHARE), jnp.bfloat16)
    bf16, f32 = jnp.bfloat16, jnp.float32
    dma = pltpu.SemaphoreType.DMA
    return pl.pallas_call(
        layer_kernel,
        out_shape=(shape, shape),
        in_specs=[anywhere] * 7,
        out_specs=(pl.BlockSpec(memory_space=pltpu.VMEM),) * 2,
        scratch_shapes=[
            pltpu.VMEM((1, NDOCS), jnp.int32),
            pltpu.VMEM((TOKENS, GROUP), bf16),
            pltpu.VMEM((TOKENS, GROUP), bf16),
            pltpu.VMEM((2, 2 * (WINDOW + TOKENS), HEAD), bf16),
            pltpu.VMEM((2, 2 * WINDOW, HEAD), f32),
            pltpu.VMEM((2, WINDOW + TOKENS, 2 * HEAD), bf16),
            pltpu.VMEM((PIECES, 2, RING, RING, 2, ROWS, PART), bf16),
            pltpu.VMEM((TOKENS, 2 * GROUP), bf16),
            pltpu.VMEM((BLOCKS, PARTS, 2, BLOCK, PART), bf16),
            pltpu.VMEM((BLOCKS, PARTS, 2, BLOCK, PART), bf16),
            pltpu.VMEM((BLOCKS, PARTS, 2, 2, BLOCK, PART), bf16),
            pltpu.VMEM((BLOCKS, PARTS, 2, 2, BLOCK, PART), bf16),
            pltpu.VMEM((BLOCKS, PARTS, 2, BLOCK, PART), f32),
            dma((3,)),
            dma((BLOCKS,)),
            dma((2,)),
            dma((2,)),
            dma((1,)),
            dma((2,)),
            dma((1,)),
            dma((PIECES,)),
            dma((1,)),
            dma((PIECES,)),
            dma((1,)),
            dma((PIECES + 1,)),
            dma((1,)),
            dma((BLOCKS, 2)),
            dma((1,)),
            dma((BLOCKS, PARTS)),
        ],
        compiler_params=pltpu.CompilerParams(
            collective_id=0, has_side_effects=True, vmem_limit_bytes=VMEM_LIMIT
        ),
        name="layer",
    )(lengths, q, qt, kv, kvt, w, wt)


def flush_kernel(a_ref, b_ref, a_hbm, b_hbm, sem):
    copies = [
        pltpu.make_async_copy(a_ref, a_hbm, sem.at[0]),
        pltpu.make_async_copy(b_ref, b_hbm, sem.at[1]),
    ]
    for copy in copies:
        copy.start()
    for copy in copies:
        copy.wait()


def flush(a, b):
    anywhere, hbm = pl.BlockSpec(memory_space=pl.ANY), pl.BlockSpec(memory_space=pltpu.HBM)
    shape = jax.ShapeDtypeStruct(a.shape, a.dtype)
    return pl.pallas_call(
        flush_kernel,
        out_shape=(shape, shape),
        in_specs=[anywhere, anywhere],
        out_specs=(hbm, hbm),
        scratch_shapes=[pltpu.SemaphoreType.DMA((2,))],
        compiler_params=pltpu.CompilerParams(vmem_limit_bytes=4 << 20),
        name="flush",
    )(a, b)


def body(
    queries, query_tangent, key_value, key_value_tangents, doc_lengths, out_weight, weight_tangent
):
    hold = lambda v: pltpu.with_memory_space_constraint(v, pltpu.HBM)
    rows = 2 * TOKENS
    out, tan = layer(
        hold(doc_lengths[None, :]),
        hold(queries),
        hold(query_tangent),
        hold(key_value.reshape(rows, HEAD)),
        hold(key_value_tangents.reshape(rows, HEAD)),
        hold(out_weight),
        hold(weight_tangent),
    )
    return flush(out, tan)


def solution(mesh):
    in_specs = (
        P("seq", "kv"),
        P("seq", "kv"),
        P("seq", None, "kv"),
        P("seq", None, "kv"),
        P(),
        P(("kv", "seq"), None),
        P(("kv", "seq"), None),
    )
    out_specs = (P("seq", "kv"), P("seq", "kv"))
    return jax.shard_map(body, mesh=mesh, in_specs=in_specs, out_specs=out_specs, check_vma=False)
```
